32 devices in a mesh: vol: 4 (over y, x), orient: 4 (over z), dp: 2 (over core).
Axes of the slice: x: 2, y: 2, z: 4, core: 2. Of those that a mesh axis runs over, the one named last changes fastest.
Arguments:
- volume: float32 [128, 65, 2, 8, 128], P('vol'), may hold values from -6 to 6
- weight_bank: float32 [64, 128, 128], replicated, may hold values from -3 to 3
- tile_slab: int32 [128, 65, 1], P(('vol', 'orient')), may hold values from 0 to 3; in each aligned block of 520 rows (0 to 519, 520 to 1039, ..., all dimensions but the last counted through in order) at most 260 rows name the same one
- tile_plane: int32 [128, 65], P(('vol', 'orient')), may hold values from 0 to 31
- tile_weight: int32 [128, 65], P(('vol', 'orient')), may hold values from 0 to 63
- particles: float32 [256, 65, 2, 128], P('dp'), may hold values from -6 to 6
- ctf: float32 [256, 65, 128], P('dp'), may hold values from -1 to 1
- noise_weight: float32 [65, 128], replicated, may hold values from 0.002 to 0.11
- offsets: int32 [256, 2], P('dp'), may hold values from -3 to 3
- earlier_class: int32 [256], P('dp'), may hold values from 0 to 7
- pose_free_term: float32 [256], P('dp'), may hold values from -160 to 160
Outputs:
- numerator: float32 [128, 65, 3, 8, 128], P(('vol', 'orient', 'dp'))
- posterior: float32 [256, 8], P('dp')
- log_evidence: float32 [256], P('dp')
The draws below stay inside these ranges and needn't reach their ends.
Inputs may be any that keep to these rules, and one draw needn't show every extreme that they name: `tile_slab`: among the 65 tiles of the 8 poses of one device at most 260 name one slab, and in every draw some device's tiles name some slab exactly 260 times.
All inputs are finite; a program needn't handle non-finite values.
Results may differ from the reference program's by a relative error of at most 0.0003.
Values sent between devices are 32-bit elements; how exact they have to be, the bound alone decides.
No kernel may reach another device: no remote copies, remote signals or barrier semaphores. Data moves between devices by JAX's collectives and lax.ppermute only.
A program may use at most 192 MiB of HBM per device.

```python
import math
import jax
import jax.numpy as jnp
import numpy as np
from jax import lax

CLASS_COUNT = 8
SIDE = 128
NT = 65
TILE = 128
BOX = 128
NW = 64
NTRANS = 9
POSE_DEV = 8
PLANES_DEV = 32
SLABS = 4
CAP = 260
POSES = 128
PARTICLES = 256


def draw_volume(key, part):
    shape = (BOX, NT, 2, CLASS_COUNT, TILE)
    return jnp.clip(jax.random.normal(jax.random.fold_in(key, 32), shape, jnp.float32), -6.0, 6.0)


def draw_weight_bank(key, part):
    shape = (NW, TILE, TILE)
    factor = 1.0 / math.sqrt(TILE)
    return factor * jnp.clip(jax.random.normal(jax.random.fold_in(key, 42), shape, jnp.float32), -6.0, 6.0)


def draw_particles(key, part):
    shape = (PARTICLES, NT, 2, TILE)
    return jnp.clip(jax.random.normal(jax.random.fold_in(key, 53), shape, jnp.float32), -6.0, 6.0)


def draw_ctf(key, part):
    base = jax.random.uniform(jax.random.fold_in(key, 11), (PARTICLES, NT, TILE), jnp.float32, -1.0, 1.0)
    return base


def draw_noise_weight(key, part):
    uniform_draw = jax.random.uniform(jax.random.fold_in(key, 21), (NT, TILE), jnp.float32, 0.0, 1.0)
    lower, upper = (math.log(0.002), math.log(0.02))
    return jnp.exp(lower + uniform_draw * (upper - lower))


def draw_pose_free_term(key, part):
    ranking = jax.random.permutation(jax.random.fold_in(key, 61), PARTICLES).astype(jnp.float32)
    spread = ranking / max(PARTICLES - 1, 1)
    jitter = jax.random.uniform(jax.random.fold_in(key, 62), (PARTICLES,), jnp.float32, -8.0, 8.0)
    return jnp.clip(-140.0 + 280.0 * spread + jitter, -160.0, 160.0)


def touch_ends(values, rng, least, high):
    longest = values.shape.index(max(values.shape))
    spots = []
    for shift in (0, 1):
        where = [jax.random.randint(jax.random.fold_in(rng, axis), (), 0, length) for axis, length in enumerate(values.shape)]
        where[longest] = (where[longest] + shift) % values.shape[longest]
        spots.append(tuple(where))
    return values.at[spots[0]].set(least).at[spots[1]].set(high)


def shared_out(stream_key, own, number, rows, amount, top, most, skew):
    order = jax.random.permutation(stream_key, amount)
    packed, usual = shares(amount, rows * top, most, skew, True), shares(amount, rows * top, most, skew, False)
    places = jnp.arange(amount)

    def named(sizes, rotation):
        used = int((sizes > 0).sum())
        fixed = max(1, used // 4)
        passed = fixed + (places - fixed + rotation * (used - fixed)) % max(1, amount - fixed)
        return jnp.zeros((amount,), jnp.int32).at[order[jnp.where(places < fixed, places, passed)]].set(jnp.asarray(sizes, jnp.int32))

    sizes = jnp.where(number % 4 == 0, named(packed, number // 4), named(usual, number - number // 4 - 1))
    mixed = jax.random.permutation(jax.random.fold_in(own, 3), amount)
    giver, taker = mixed[0:amount // 2 * 2:2], mixed[1:amount // 2 * 2:2]
    margin = jnp.minimum(sizes[giver] - 1, most - sizes[taker]) // 2
    margin = jnp.where((giver == order[0]) | (taker == order[0]) | (sizes[taker] == 0), 0, jnp.maximum(margin, 0))
    passed = jax.random.randint(jax.random.fold_in(own, 4), (amount // 2,), 0, 1 << 20) % (margin + 1)
    sizes = sizes.at[giver].add(-passed).at[taker].add(passed)
    labels = jnp.searchsorted(jnp.cumsum(sizes), jnp.arange(rows * top), side="right").astype(jnp.int32)
    listing = labels.reshape(top, rows).T
    listing = listing[jax.random.permutation(jax.random.fold_in(own, 1), rows)]
    rotation = jax.random.randint(jax.random.fold_in(own, 2), (rows, 1), 0, top)
    return jnp.take_along_axis(listing, (jnp.arange(top)[None, :] + rotation) % top, axis=1)


def shares(count, total, reach, lean, full):
    loads = [(1 << 20) // math.isqrt(rank ** lean) + 1 for rank in range(1, count + 1)]
    largest = reach if full else min(reach, max(-(-total // count), total * loads[0] // sum(loads)))
    least = 1 if total - largest >= count - 1 else 0
    given, rest = [largest] + [least] * (count - 1), total - largest - least * (count - 1)
    while rest > 0:
        movable = [i for i in range(1, count) if given[i] < largest] or [i for i in range(1, count) if given[i] < reach]
        pool, left = sum([loads[i] for i in movable]), rest
        for i in movable:
            more = min(reach - given[i], max(1, left * loads[i] // pool), rest)
            given[i] = given[i] + more
            rest = rest - more
    return np.array(given)


def setup_inputs(seed: int = 0) -> dict:
    key_list = jax.random.split(jax.random.key(seed), 12)
    volume = draw_volume(jax.random.fold_in(key_list[11], 71), 0)
    weight_bank = draw_weight_bank(jax.random.fold_in(key_list[11], 71), 0)
    tile_slab_keys = jax.random.split(jax.random.fold_in(key_list[2], 1), POSES * NT // (POSE_DEV * NT))
    tile_slab_turns = jax.random.permutation(jax.random.fold_in(key_list[2], 3), POSES * NT // (POSE_DEV * NT))
    tile_slab = jax.vmap(lambda own, number: shared_out(jax.random.fold_in(key_list[2], 2), own, number, POSE_DEV * NT, SLABS, 1, CAP, 2))(tile_slab_keys, tile_slab_turns).reshape((POSES, NT, 1))
    tile_plane = touch_ends(jax.random.randint(key_list[3], (POSES, NT), 0, PLANES_DEV), jax.random.fold_in(key_list[3], 1), 0, PLANES_DEV - 1).astype(jnp.int32)
    tile_weight = touch_ends(jax.random.randint(key_list[4], (POSES, NT), 0, NW), jax.random.fold_in(key_list[4], 1), 0, NW - 1).astype(jnp.int32)
    particles = draw_particles(jax.random.fold_in(key_list[11], 71), 0)
    ctf = draw_ctf(jax.random.fold_in(key_list[11], 71), 0)
    noise_weight = draw_noise_weight(jax.random.fold_in(key_list[11], 71), 0)
    offsets = touch_ends(jax.random.randint(key_list[8], (PARTICLES, 2), -3, 4), jax.random.fold_in(key_list[8], 1), -3, 3).astype(jnp.int32)
    earlier_class = touch_ends(jax.random.randint(key_list[9], (PARTICLES,), 0, CLASS_COUNT), jax.random.fold_in(key_list[9], 1), 0, CLASS_COUNT - 1).astype(jnp.int32)
    pose_free_term = draw_pose_free_term(jax.random.fold_in(key_list[11], 71), 0)
    return dict(volume=volume, weight_bank=weight_bank, tile_slab=tile_slab, tile_plane=tile_plane, tile_weight=tile_weight, particles=particles, ctf=ctf, noise_weight=noise_weight, offsets=offsets, earlier_class=earlier_class, pose_free_term=pose_free_term)


PREVIOUS_REWARD = 1.5
PRECISE = lax.Precision.HIGHEST


def pixel_frequencies(image_side, tile_count, tile_width):
    pixel = jnp.arange(tile_count * tile_width, dtype=jnp.int32).reshape(tile_count, tile_width)
    half_width = image_side // 2 + 1
    freq_x = pixel % half_width
    row_index = pixel // half_width
    freq_y = jnp.where(row_index < image_side // 2, row_index, row_index - image_side)
    return freq_x, freq_y


def moved_images(images, offsets, freq_x, freq_y, image_side, trans_step):
    shift_horizontal = offsets[:, 0] + (trans_step % 3 - 1)
    move_y = offsets[:, 1] + (trans_step // 3 - 1)
    turns = jnp.mod(freq_x[None] * shift_horizontal[:, None, None] + freq_y[None] * move_y[:, None, None], image_side)
    phase_angle = turns.astype(jnp.float32) * (2.0 * math.pi / image_side)
    cosine = jnp.cos(phase_angle)
    sine_part = jnp.sin(phase_angle)
    real_part = images[:, :, 0, :]
    imag_part = images[:, :, 1, :]
    return jnp.stack([real_part * cosine + imag_part * sine_part, imag_part * cosine - real_part * sine_part], axis=2)


def project_tiles(blocks, weight_bank, chosen):
    matrices = weight_bank[chosen]
    return jnp.einsum('nckr,nrq->nckq', blocks, matrices, precision=PRECISE)


def back_project(tile_rows, weight_bank, chosen):
    matrices = weight_bank[chosen]
    return jnp.einsum('nmkq,nrq->nmkr', tile_rows, matrices, precision=PRECISE)


def reference(volume, weight_bank, tile_slab, tile_plane, tile_weight, particles, ctf, noise_weight, offsets, earlier_class, pose_free_term):
    freq_x, freq_y = pixel_frequencies(SIDE, NT, TILE)
    segment = jnp.arange(NT, dtype=jnp.int32)
    planes_of = (tile_slab[:, :, 0] * PLANES_DEV + tile_plane).astype(jnp.int32)
    groups = POSES // POSE_DEV
    plane_groups = planes_of.reshape(groups, POSE_DEV, NT)
    weight_groups = tile_weight.reshape(groups, POSE_DEV, NT)
    ctf_noise = noise_weight[None] * ctf
    trans_steps = jnp.arange(NTRANS, dtype=jnp.int32)

    def move_one(trans_step):
        return moved_images(particles, offsets, freq_x, freq_y, SIDE, trans_step)

    moved = lax.map(move_one, trans_steps)
    weighted = ctf_noise[None, :, :, None, :] * moved
    earlier_class_term = jnp.where(earlier_class[:, None] == jnp.arange(CLASS_COUNT, dtype=jnp.int32)[None], PREVIOUS_REWARD, 0.0)
    earlier_class_term = earlier_class_term + pose_free_term[:, None]

    def slices_of(plane_rows, chosen_rows):
        def single_orientation(pair_items):
            return project_tiles(volume[pair_items[0], segment], weight_bank, pair_items[1])
        return lax.map(single_orientation, (plane_rows, chosen_rows))

    def group_scores(pair_items):
        slices = slices_of(pair_items[0], pair_items[1])
        power = jnp.sum(slices * slices, axis=2)
        norm_term = jnp.einsum('itq,ptkq->ikp', ctf_noise * ctf, power, precision=PRECISE)
        cross_term = jnp.einsum('jitcq,ptckq->jikp', weighted, slices, precision=PRECISE)
        return 2.0 * cross_term - norm_term[None] + earlier_class_term[None, :, :, None]

    scores = lax.map(group_scores, (plane_groups, weight_groups))
    peak_value = jnp.max(scores, axis=(0, 1, 3, 4))
    exp_scores = jnp.exp(scores - peak_value[None, None, :, None, None])
    class_mass = jnp.sum(exp_scores, axis=(0, 1, 4))
    mass_total = jnp.sum(class_mass, axis=1)
    posterior = class_mass / mass_total[:, None]
    evidence = peak_value + jnp.log(mass_total)
    post_share = exp_scores * (POSES / mass_total)[None, None, :, None, None]
    ctf_moved = ctf[None, :, :, None, :] * moved
    ctf_square = ctf * ctf

    def group_volume(running, pair_items):
        share_group, plane_rows, chosen_rows = pair_items
        data_rows = jnp.einsum('jikp,jitcq->ptckq', share_group, ctf_moved, precision=PRECISE)
        weight_rows = jnp.einsum('ikp,itq->ptkq', jnp.sum(share_group, axis=0), ctf_square, precision=PRECISE)
        slice_rows = jnp.concatenate([data_rows, weight_rows[:, :, None]], axis=2)

        def spread_pose(item_pair):
            return back_project(item_pair[0], weight_bank, item_pair[1])

        scatter_weights = lax.map(spread_pose, (slice_rows, chosen_rows))
        cell_index = (plane_rows * NT + segment[None]).reshape(-1).astype(jnp.int32)
        return running.at[cell_index].add(scatter_weights.reshape(-1, 3, CLASS_COUNT, TILE)), None

    start = jnp.zeros((BOX * NT, 3, CLASS_COUNT, TILE), jnp.float32)
    numerator = lax.scan(group_volume, start, (post_share, plane_groups, weight_groups))[0]
    return numerator.reshape(BOX, NT, 3, CLASS_COUNT, TILE), posterior, evidence
```

```python
import math

import jax
import jax.numpy as jnp
import numpy as np
from jax import lax
from jax.experimental import pallas as pl
from jax.experimental.pallas import tpu as pltpu
from jax.sharding import PartitionSpec as P

SIDE = 128
NTRANS = 9
REACH = 3
PREVIOUS_REWARD = 1.5
CHUNK = 8
F32 = jnp.float32
BF16 = jnp.bfloat16


def phase_tables(tile_count, tile_width):
    pixel = np.arange(tile_count * tile_width).reshape(tile_count, tile_width)
    half_width = SIDE // 2 + 1
    freq_x = pixel % half_width
    row = pixel // half_width
    freq_y = np.where(row < SIDE // 2, row, row - SIDE)

    def pair(freq, steps):
        turns = np.mod(freq[:, None, :] * np.asarray(steps)[None, :, None], SIDE)
        angle = turns * (2.0 * math.pi / SIDE)
        return np.concatenate([np.cos(angle), np.sin(angle)], axis=2)

    steps = list(range(-REACH, REACH + 1)) + [0]
    prior = np.concatenate([pair(freq_x, steps), pair(freq_y, steps)], axis=1)
    j = np.arange(NTRANS)
    turns = np.mod(
        freq_x[:, None, :] * (j % 3 - 1)[None, :, None] + freq_y[:, None, :] * (j // 3 - 1)[None, :, None],
        SIDE,
    )
    angle = turns * (2.0 * math.pi / SIDE)
    step = np.stack([np.cos(angle), np.sin(angle)], axis=1)
    return prior.astype(np.float32), step.astype(np.float32)


def divisor(count, most):
    return max(d for d in range(1, most + 1) if count % d == 0)


def split(x):
    high = x.astype(BF16)
    return high, (x - high.astype(F32)).astype(BF16)


def rounded(x):
    high = lax.reduce_precision(x, 8, 7)
    return high.astype(BF16), (x - high).astype(BF16)


def halves_sum(r):
    m, n = r.shape[0] // 2, r.shape[1] // 2
    return (r[:m, :n] + r[m:, :n]) + (r[:m, n:] + r[m:, n:])


def bits_of(count):
    return max(1, (count - 1).bit_length())


def compact(mask, code, spare):
    poses = mask.shape[0]
    order = jnp.arange(poses, dtype=jnp.int32)
    before = (order[:, None] > order[None, :]).astype(BF16)
    rank = jnp.dot(before, mask.astype(BF16), preferred_element_type=F32).astype(jnp.int32)
    rank = jnp.where(mask, rank, -1)
    hit = rank[None, :, :] == order[:, None, None]
    listing = jnp.sum(jnp.where(hit, (code - spare)[None], 0), axis=1) + spare
    return listing.T.reshape(-1), jnp.sum(mask.astype(jnp.int32), axis=0)


def prepare_kernel(x_ref, ctf_ref, pick_x_ref, pick_y_ref, prior_ref, y_ref, square_ref):
    count = x_ref.shape[0]
    width = x_ref.shape[3]
    particles = x_ref.shape[2]
    options = pick_x_ref.shape[1]
    for tt in range(count):
        ex = jnp.dot(pick_x_ref[...], prior_ref[tt, :options], precision=lax.Precision.HIGHEST, preferred_element_type=F32)
        ey = jnp.dot(pick_y_ref[...], prior_ref[tt, options:], precision=lax.Precision.HIGHEST, preferred_element_type=F32)
        cx, sx, cy, sy = ex[:, :width], ex[:, width:], ey[:, :width], ey[:, width:]
        cosine = cx * cy - sx * sy
        sine = sx * cy + cx * sy
        ctf = ctf_ref[tt]
        real, imag = x_ref[tt, 0] * ctf, x_ref[tt, 1] * ctf
        moved = jnp.concatenate([real * cosine + imag * sine, imag * cosine - real * sine], axis=1)
        high, low = split(moved)
        y_ref[tt, :particles, :] = high
        y_ref[tt, particles:, :] = low
        high, low = split(ctf * ctf)
        square_ref[tt, :particles, :] = high
        square_ref[tt, particles:, :] = low


def prepare(x, ctf, pick_x, pick_y, prior, block):
    tiles, _, particles, width = x.shape
    options = pick_x.shape[1]
    return pl.pallas_call(
        prepare_kernel,
        grid=(tiles // block,),
        in_specs=[
            pl.BlockSpec((block, 2, particles, width), lambda t: (t, 0, 0, 0)),
            pl.BlockSpec((block, particles, width), lambda t: (t, 0, 0)),
            pl.BlockSpec((particles, options), lambda t: (0, 0)),
            pl.BlockSpec((particles, options), lambda t: (0, 0)),
            pl.BlockSpec((block, 2 * options, 2 * width), lambda t: (t, 0, 0)),
        ],
        out_specs=[
            pl.BlockSpec((block, 2 * particles, 2 * width), lambda t: (t, 0, 0)),
            pl.BlockSpec((block, 2 * particles, width), lambda t: (t, 0, 0)),
        ],
        out_shape=[
            jax.ShapeDtypeStruct((tiles, 2 * particles, 2 * width), BF16),
            jax.ShapeDtypeStruct((tiles, 2 * particles, width), BF16),
        ],
        compiler_params=pltpu.CompilerParams(vmem_limit_bytes=40 << 20),
        cost_estimate=pl.CostEstimate(flops=tiles * particles * width * 100, bytes_accessed=tiles * particles * width * 24, transcendentals=0),
        name="prepare",
    )(x, ctf, pick_x, pick_y, prior)


NT_DIMS = (((1,), (1,)), ((), ()))


def score_kernel(weight_bits, plane_bits, count_ref, list_ref, volume_ref, weight_ref, y_ref, square_ref, step_ref, noise_ref, out_ref, acc):
    block = pl.program_id(0)
    tiles = y_ref.shape[0]
    width = square_ref.shape[2]
    classes = volume_ref.shape[3]
    poses = out_ref.shape[0]

    @pl.when(block == 0)
    def _():
        acc[...] = jnp.zeros_like(acc)

    def tile(tt, carry):
        t = block * tiles + tt

        def chunk(c, carry):
            pose, real, imag = [], [], []
            for s in range(CHUNK):
                code = list_ref[t * poses + c * CHUNK + s]
                chosen = code & ((1 << weight_bits) - 1)
                plane = (code >> weight_bits) & ((1 << plane_bits) - 1)
                pose.append(code >> (weight_bits + plane_bits))
                high, low = split(volume_ref[plane, tt].reshape(2 * classes, width))
                r = jnp.dot(jnp.concatenate([high, low], axis=0), weight_ref[chosen], preferred_element_type=F32)
                r = halves_sum(r)
                real.append(r[:classes])
                imag.append(r[classes:])
            real, imag = jnp.concatenate(real, axis=0), jnp.concatenate(imag, axis=0)
            noise = noise_ref[tt]
            high, low = split((real * real + imag * imag) * noise)
            r = lax.dot_general(jnp.concatenate([high, low], axis=0), square_ref[tt], NT_DIMS, preferred_element_type=F32)
            norm = halves_sum(r)
            real, imag = real * (2.0 * noise), imag * (2.0 * noise)
            for j in range(NTRANS):
                cosine, sine = step_ref[tt, 0, j : j + 1, :], step_ref[tt, 1, j : j + 1, :]
                turned = jnp.concatenate([real * cosine - imag * sine, real * sine + imag * cosine], axis=1)
                high, low = split(turned)
                r = lax.dot_general(jnp.concatenate([high, low], axis=0), y_ref[tt], NT_DIMS, preferred_element_type=F32)
                r = halves_sum(r) - norm
                n = r.shape[1]
                for s in range(CHUNK):
                    acc[pose[s], :, j * n : (j + 1) * n] += r[s * classes : (s + 1) * classes]
            return carry

        return lax.fori_loop(0, (count_ref[t] + CHUNK - 1) // CHUNK, chunk, carry)

    lax.fori_loop(0, tiles, tile, 0)

    @pl.when(block == pl.num_programs(0) - 1)
    def _():
        out_ref[...] = acc[:poses]


def partial_scores(counts, listing, volume, weights, y, square, step, noise, poses, block):
    planes, tiles, _, classes, width = volume.shape
    particles = y.shape[1] // 2
    bank = weights.shape[0]
    grid_spec = pltpu.PrefetchScalarGridSpec(
        num_scalar_prefetch=2,
        grid=(tiles // block,),
        in_specs=[
            pl.BlockSpec((planes, block, 2, classes, width), lambda t, *_: (0, t, 0, 0, 0)),
            pl.BlockSpec(weights.shape, lambda t, *_: (0, 0, 0), pipeline_mode=pl.Buffered(1)),
            pl.BlockSpec((block, 2 * particles, 2 * width), lambda t, *_: (t, 0, 0)),
            pl.BlockSpec((block, 2 * particles, width), lambda t, *_: (t, 0, 0)),
            pl.BlockSpec((block, 2, NTRANS, width), lambda t, *_: (t, 0, 0, 0)),
            pl.BlockSpec((block, 1, width), lambda t, *_: (t, 0, 0)),
        ],
        out_specs=pl.BlockSpec((poses, classes, NTRANS * particles), lambda t, *_: (0, 0, 0)),
        scratch_shapes=[pltpu.VMEM((poses + 1, classes, NTRANS * particles), F32)],
    )

    def body(*refs):
        score_kernel(bits_of(bank), bits_of(planes), *refs)

    return pl.pallas_call(
        body,
        grid_spec=grid_spec,
        out_shape=jax.ShapeDtypeStruct((poses, classes, NTRANS * particles), F32),
        compiler_params=pltpu.CompilerParams(vmem_limit_bytes=56 << 20),
        name="score",
    )(counts, listing, volume, weights, y, square, step, noise)


def spread_kernel(weight_bits, plane_bits, count_ref, list_ref, score_ref, term_ref, weight_ref, y_ref, square_ref, step_ref,
                  own_ref, other_ref, posterior_ref, evidence_ref, share, acc):
    block = pl.program_id(0)
    tiles = y_ref.shape[0]
    width = square_ref.shape[2]
    poses, classes = score_ref.shape[0], score_ref.shape[1]
    n = term_ref.shape[1]
    half = own_ref.shape[0]

    @pl.when(block == 0)
    def _():
        term = term_ref[...]

        def largest(p, best):
            for j in range(NTRANS):
                best = jnp.maximum(best, score_ref[p, :, j * n : (j + 1) * n] + term)
            return best

        best = lax.fori_loop(0, poses, largest, jnp.full((classes, n), -jnp.inf, F32))
        peak = jnp.max(best, axis=0, keepdims=True)

        def mass(p, total):
            for j in range(NTRANS):
                total = total + jnp.exp((score_ref[p, :, j * n : (j + 1) * n] + term) - peak)
            return total

        class_mass = lax.fori_loop(0, poses, mass, jnp.zeros((classes, n), F32))
        total = jnp.sum(class_mass, axis=0, keepdims=True)
        posterior_ref[...] = class_mass / total
        evidence_ref[...] = peak + jnp.log(total)
        factor = jnp.broadcast_to(poses / total, (classes, n))

        def normal(p, carry):
            every = jnp.zeros((classes, n), F32)
            for j in range(NTRANS):
                e = jnp.exp((score_ref[p, :, j * n : (j + 1) * n] + term) - peak) * factor
                every = every + e
                high = e.astype(BF16).astype(F32)
                share[p, :, j * n : (j + 1) * n] = jnp.concatenate([high, e - high], axis=0).astype(BF16)
            high = every.astype(BF16).astype(F32)
            share[p, :, NTRANS * n :] = jnp.concatenate([high, every - high], axis=0).astype(BF16)
            return carry

        lax.fori_loop(0, poses, normal, 0)

    def pairs(r):
        return [r[2 * s * classes : (2 * s + 1) * classes] + r[(2 * s + 1) * classes : (2 * s + 2) * classes] for s in range(CHUNK)]

    def tile(tt, carry):
        t = block * tiles + tt
        acc[...] = jnp.zeros_like(acc)

        def chunk(c, carry):
            pose, plane, chosen = [], [], []
            for s in range(CHUNK):
                code = list_ref[t * poses + c * CHUNK + s]
                chosen.append(code & ((1 << weight_bits) - 1))
                plane.append((code >> weight_bits) & ((1 << plane_bits) - 1))
                pose.append(code >> (weight_bits + plane_bits))
            real = jnp.zeros((CHUNK * classes, width), F32)
            imag = jnp.zeros((CHUNK * classes, width), F32)
            for j in range(NTRANS):
                rows = jnp.concatenate([share[pose[s], :, j * n : (j + 1) * n] for s in range(CHUNK)], axis=0)
                r = jnp.dot(jnp.concatenate([rows, rows], axis=1), y_ref[tt], preferred_element_type=F32)
                r = jnp.concatenate(pairs(r), axis=0)
                cosine, sine = step_ref[tt, 0, j : j + 1, :], step_ref[tt, 1, j : j + 1, :]
                real = real + (r[:, :width] * cosine + r[:, width:] * sine)
                imag = imag + (r[:, width:] * cosine - r[:, :width] * sine)
            rows = jnp.concatenate([share[pose[s], :, NTRANS * n :] for s in range(CHUNK)], axis=0)
            r = jnp.dot(jnp.concatenate([rows, rows], axis=1), square_ref[tt], preferred_element_type=F32)
            power = pairs(r)
            for s in range(CHUNK):
                where = slice(s * classes, (s + 1) * classes)
                rows = jnp.concatenate([real[where], imag[where], power[s]], axis=0)
                high = rows.astype(BF16).astype(F32)
                both = jnp.concatenate([high, rows - high], axis=0).astype(BF16)
                r = jnp.dot(both, weight_ref[chosen[s]], preferred_element_type=F32)
                acc[plane[s]] += halves_sum(r)
            return carry

        lax.fori_loop(0, (count_ref[t] + CHUNK - 1) // CHUNK, chunk, 0)
        own_ref[:, tt] = acc[:half].reshape(half, 3, classes, width)
        other_ref[:, tt] = acc[half : 2 * half].reshape(half, 3, classes, width)
        return carry

    lax.fori_loop(0, tiles, tile, 0)


def spread(counts, listing, scores, term, weights, y, square, step, planes, block):
    poses, classes, _ = scores.shape
    tiles, particles, width = square.shape[0], square.shape[1] // 2, square.shape[2]
    bank = weights.shape[0]
    half = planes // 2
    part = pl.BlockSpec((half, block, 3, classes, width), lambda t, *_: (0, t, 0, 0, 0))
    grid_spec = pltpu.PrefetchScalarGridSpec(
        num_scalar_prefetch=2,
        grid=(tiles // block,),
        in_specs=[
            pl.BlockSpec(scores.shape, lambda t, *_: (0, 0, 0), pipeline_mode=pl.Buffered(1)),
            pl.BlockSpec(term.shape, lambda t, *_: (0, 0)),
            pl.BlockSpec(weights.shape, lambda t, *_: (0, 0, 0), pipeline_mode=pl.Buffered(1)),
            pl.BlockSpec((block, 2 * particles, 2 * width), lambda t, *_: (t, 0, 0)),
            pl.BlockSpec((block, 2 * particles, width), lambda t, *_: (t, 0, 0)),
            pl.BlockSpec((block, 2, NTRANS, width), lambda t, *_: (t, 0, 0, 0)),
        ],
        out_specs=[part, part, pl.BlockSpec((classes, particles), lambda t, *_: (0, 0)), pl.BlockSpec((1, particles), lambda t, *_: (0, 0))],
        scratch_shapes=[
            pltpu.VMEM((poses, 2 * classes, (NTRANS + 1) * particles), BF16),
            pltpu.VMEM((planes + 1, 3 * classes, width), F32),
        ],
    )

    def body(*refs):
        spread_kernel(bits_of(bank), bits_of(planes + 1), *refs)

    shape = jax.ShapeDtypeStruct((half, tiles, 3, classes, width), F32)
    return pl.pallas_call(
        body,
        grid_spec=grid_spec,
        out_shape=[shape, shape, jax.ShapeDtypeStruct((classes, particles), F32), jax.ShapeDtypeStruct((1, particles), F32)],
        compiler_params=pltpu.CompilerParams(vmem_limit_bytes=58 << 20),
        name="spread",
    )(counts, listing, scores, term, weights, y, square, step)


def shards(volume, weight_bank, tile_slab, tile_plane, tile_weight, particles, ctf, noise_weight, offsets, earlier_class, pose_free_term):
    slabs, orients, parts = lax.axis_size("vol"), lax.axis_size("orient"), lax.axis_size("dp")
    slab, orient, part = lax.axis_index("vol"), lax.axis_index("orient"), lax.axis_index("dp")
    planes, tiles, _, classes, width = volume.shape
    bank = weight_bank.shape[0]
    local_poses = tile_plane.shape[0]
    group = slabs * local_poses
    block = divisor(tiles, 5)

    named = jnp.stack([tile_slab[:, :, 0], tile_plane, tile_weight])
    named = lax.all_gather(named, ("vol", "orient"))

    prior, step = phase_tables(tiles, width)
    options = prior.shape[1] // 2
    pick = [(offsets[:, axis : axis + 1] + REACH == jnp.arange(options, dtype=jnp.int32)[None]).astype(F32) for axis in (0, 1)]
    y, square = prepare(particles.transpose(1, 2, 0, 3), ctf.transpose(1, 0, 2), pick[0], pick[1], prior, block)
    high, low = rounded(weight_bank)
    ahead = jnp.concatenate([high, low], axis=2)
    high, low = rounded(weight_bank.transpose(0, 2, 1))
    back = jnp.concatenate([high, low], axis=2)

    weight_bits = bits_of(bank)
    named = named.reshape(slabs, orients, 3, local_poses, tiles)
    own = lax.dynamic_index_in_dim(named, orient, axis=1, keepdims=False)
    own = own.transpose(1, 0, 2, 3).reshape(3, group, tiles)
    pose = jnp.arange(group, dtype=jnp.int32)[:, None]
    shift = weight_bits + bits_of(planes)
    code = (pose << shift) | (own[1] << weight_bits) | own[2]
    listing, counts = compact(own[0] == slab, code, group << shift)

    every = named.transpose(2, 0, 1, 3, 4).reshape(3, slabs * orients * local_poses, tiles)
    reach = planes // orients
    half = reach // parts
    pose = jnp.arange(every.shape[1], dtype=jnp.int32)[:, None]
    place = jnp.mod(every[1] - orient * reach - part * half, reach)
    shift = weight_bits + bits_of(reach + 1)
    code = (pose << shift) | (place << weight_bits) | every[2]
    mask = (every[0] == slab) & (every[1] // reach == orient)
    back_listing, back_counts = compact(mask, code, reach << weight_bits)

    scores = partial_scores(counts, listing, volume, ahead, y, square, step, noise_weight[:, None, :], group, block)
    scores = lax.psum_scatter(scores, "vol", scatter_dimension=0, tiled=True)
    scores = lax.all_gather(scores, ("vol", "orient"), tiled=True)

    term = jnp.where(earlier_class[None, :] == jnp.arange(classes, dtype=jnp.int32)[:, None], PREVIOUS_REWARD, 0.0)
    term = term + pose_free_term[None, :]
    mine, other, posterior, evidence = spread(back_counts, back_listing, scores, term, back, y, square, step, reach, block)
    numerator = mine + lax.ppermute(other, "dp", [(0, 1), (1, 0)])
    return numerator, posterior.T, evidence[0]


def solution(mesh):
    in_specs = (
        P("vol", None, None, None, None),
        P(),
        P(("vol", "orient"), None, None),
        P(("vol", "orient"), None),
        P(("vol", "orient"), None),
        P("dp", None, None, None),
        P("dp", None, None),
        P(),
        P("dp", None),
        P("dp"),
        P("dp"),
    )
    out_specs = (P(("vol", "orient", "dp"), None, None, None, None), P("dp", None), P("dp"))
    return jax.shard_map(shards, mesh=mesh, in_specs=in_specs, out_specs=out_specs, check_vma=False)
```

```python
import math

import jax
import jax.numpy as jnp
import numpy as np
from jax import lax
from jax.experimental import pallas as pl
from jax.experimental.pallas import tpu as pltpu
from jax.sharding import PartitionSpec as P

SIDE = 128
NTRANS = 9
REACH = 3
PREVIOUS_REWARD = 1.5
CHUNK = 8
TOGETHER = 9
F32 = jnp.float32
BF16 = jnp.bfloat16


def phase_tables(tile_count, tile_width):
    pixel = np.arange(tile_count * tile_width).reshape(tile_count, tile_width)
    half_width = SIDE // 2 + 1
    freq_x = pixel % half_width
    row = pixel // half_width
    freq_y = np.where(row < SIDE // 2, row, row - SIDE)

    def pair(freq, steps):
        turns = np.mod(freq[:, None, :] * np.asarray(steps)[None, :, None], SIDE)
        angle = turns * (2.0 * math.pi / SIDE)
        return np.concatenate([np.cos(angle), np.sin(angle)], axis=2)

    steps = list(range(-REACH, REACH + 1)) + [0]
    prior = np.concatenate([pair(freq_x, steps), pair(freq_y, steps)], axis=1)
    j = np.arange(NTRANS)
    turns = np.mod(
        freq_x[:, None, :] * (j % 3 - 1)[None, :, None] + freq_y[:, None, :] * (j // 3 - 1)[None, :, None],
        SIDE,
    )
    angle = turns * (2.0 * math.pi / SIDE)
    step = np.stack([np.cos(angle), np.sin(angle)], axis=1)
    return prior.astype(np.float32), step.astype(np.float32)


def divisor(count, most):
    return max(d for d in range(1, most + 1) if count % d == 0)


def split(x):
    high = x.astype(BF16)
    return high, (x - high.astype(F32)).astype(BF16)


def rounded(x):
    high = lax.reduce_precision(x, 8, 7)
    return high.astype(BF16), (x - high).astype(BF16)


def halves_sum(r):
    m, n = r.shape[0] // 2, r.shape[1] // 2
    return (r[:m, :n] + r[m:, :n]) + (r[:m, n:] + r[m:, n:])


def bits_of(count):
    return max(1, (count - 1).bit_length())


def compact(mask, code, spare):
    poses = mask.shape[0]
    order = jnp.arange(poses, dtype=jnp.int32)
    before = (order[:, None] > order[None, :]).astype(BF16)
    rank = jnp.dot(before, mask.astype(BF16), preferred_element_type=F32).astype(jnp.int32)
    rank = jnp.where(mask, rank, -1)
    hit = rank[None, :, :] == order[:, None, None]
    listing = jnp.sum(jnp.where(hit, (code - spare)[None], 0), axis=1) + spare
    return listing.T.reshape(-1), jnp.sum(mask.astype(jnp.int32), axis=0)


def chunk_table(counts, poses, block):
    chunks = ((counts + CHUNK - 1) // CHUNK).reshape(-1, block)
    place = jnp.arange(block, dtype=jnp.int32)
    end = jnp.sum(jnp.where(place[:, None] <= place[None, :], chunks[:, :, None], 0), axis=1)
    g = jnp.arange(block * poses // CHUNK, dtype=jnp.int32)[None, :, None]
    tile = jnp.minimum(jnp.sum((g >= end[:, None, :]).astype(jnp.int32), axis=2), block - 1)
    first = jnp.sum(jnp.where(place == tile[:, :, None], (end - chunks)[:, None, :], 0), axis=2)
    step = jnp.minimum(jnp.maximum(g[:, :, 0] - first, 0), poses // CHUNK - 1)
    start = (jnp.arange(chunks.shape[0], dtype=jnp.int32)[:, None] * block + tile) * poses + step * CHUNK
    return ((start << bits_of(block)) | tile).reshape(-1), end[:, -1]


def prepare_kernel(turned, x_ref, ctf_ref, pick_x_ref, pick_y_ref, prior_ref, y_ref, square_ref):
    count = x_ref.shape[0]
    width = x_ref.shape[3]
    particles = x_ref.shape[2]
    options = pick_x_ref.shape[1]
    for tt in range(count):
        ex = jnp.dot(pick_x_ref[...], prior_ref[tt, :options], precision=lax.Precision.HIGHEST, preferred_element_type=F32)
        ey = jnp.dot(pick_y_ref[...], prior_ref[tt, options:], precision=lax.Precision.HIGHEST, preferred_element_type=F32)
        cx, sx, cy, sy = ex[:, :width], ex[:, width:], ey[:, :width], ey[:, width:]
        cosine = cx * cy - sx * sy
        sine = sx * cy + cx * sy
        ctf = ctf_ref[tt]
        real, imag = x_ref[tt, 0] * ctf, x_ref[tt, 1] * ctf
        moved = jnp.concatenate([real * cosine + imag * sine, imag * cosine - real * sine], axis=1)
        for source, target in ((moved, y_ref), (ctf * ctf, square_ref)):
            if turned:
                high, low = split(source.T)
                target[tt, :, :particles] = high
                target[tt, :, particles:] = low
            else:
                high, low = split(source)
                target[tt, :particles, :] = high
                target[tt, particles:, :] = low


def prepare(x, ctf, pick_x, pick_y, prior, block, turned):
    tiles, _, particles, width = x.shape
    options = pick_x.shape[1]
    shapes = [(2 * width, 2 * particles), (width, 2 * particles)] if turned else [(2 * particles, 2 * width), (2 * particles, width)]
    return pl.pallas_call(
        lambda *refs: prepare_kernel(turned, *refs),
        grid=(tiles // block,),
        in_specs=[
            pl.BlockSpec((block, 2, particles, width), lambda t: (t, 0, 0, 0)),
            pl.BlockSpec((block, particles, width), lambda t: (t, 0, 0)),
            pl.BlockSpec((particles, options), lambda t: (0, 0)),
            pl.BlockSpec((particles, options), lambda t: (0, 0)),
            pl.BlockSpec((block, 2 * options, 2 * width), lambda t: (t, 0, 0)),
        ],
        out_specs=[pl.BlockSpec((block, *shape), lambda t: (t, 0, 0)) for shape in shapes],
        out_shape=[jax.ShapeDtypeStruct((tiles, *shape), BF16) for shape in shapes],
        compiler_params=pltpu.CompilerParams(vmem_limit_bytes=40 << 20),
        cost_estimate=pl.CostEstimate(flops=tiles * particles * width * 100, bytes_accessed=tiles * particles * width * 24, transcendentals=0),
        name="prepare",
    )(x, ctf, pick_x, pick_y, prior)


def score_kernel(weight_bits, plane_bits, total_ref, table_ref, list_ref, volume_ref, weight_ref, y_ref, square_ref, step_ref, noise_ref, out_ref, acc):
    block = pl.program_id(0)
    tiles = y_ref.shape[0]
    width = square_ref.shape[1]
    n = square_ref.shape[2] // 2
    classes = volume_ref.shape[3]
    poses = out_ref.shape[0]
    rows = CHUNK * classes
    most = tiles * poses // CHUNK
    total = total_ref[block]

    @pl.when(block == 0)
    def _():
        acc[...] = jnp.zeros_like(acc)

    def entry(g):
        code = table_ref[block * most + g]
        return code >> bits_of(tiles), code & ((1 << bits_of(tiles)) - 1)

    def project(g):
        start, tt = entry(g)
        real, imag = [], []
        for s in range(CHUNK):
            code = list_ref[start + s]
            chosen = code & ((1 << weight_bits) - 1)
            plane = (code >> weight_bits) & ((1 << plane_bits) - 1)
            high, low = split(volume_ref[plane, tt].reshape(2 * classes, width))
            r = halves_sum(jnp.dot(jnp.concatenate([high, low], axis=0), weight_ref[chosen], preferred_element_type=F32))
            real.append(r[:classes])
            imag.append(r[classes:])
        return jnp.concatenate(real, axis=0), jnp.concatenate(imag, axis=0)

    def chunk(g, slices):
        real, imag = slices
        following = project(jnp.minimum(g + 1, total - 1))
        start, tt = entry(g)
        pose = [list_ref[start + s] >> (weight_bits + plane_bits) for s in range(CHUNK)]
        noise = noise_ref[tt]
        high, low = split((real * real + imag * imag) * noise)
        norm = halves_sum(jnp.dot(jnp.concatenate([high, low], axis=0), square_ref[tt], preferred_element_type=F32))
        real, imag = real * (2.0 * noise), imag * (2.0 * noise)
        turned = []
        for j in range(NTRANS):
            cosine, sine = step_ref[tt, 0, j : j + 1, :], step_ref[tt, 1, j : j + 1, :]
            turned += split(jnp.concatenate([real * cosine - imag * sine, real * sine + imag * cosine], axis=1))
        r = jnp.dot(jnp.concatenate(turned, axis=0), y_ref[tt], preferred_element_type=F32)
        before = [acc[pose[s]] for s in range(CHUNK)]
        part = jnp.concatenate([halves_sum(r[2 * j * rows : 2 * (j + 1) * rows]) - norm for j in range(NTRANS)], axis=1)
        for s in range(CHUNK):
            acc[pose[s]] = before[s] + part[s * classes : (s + 1) * classes]
        return following

    lax.fori_loop(0, total, chunk, project(0))

    @pl.when(block == pl.num_programs(0) - 1)
    def _():
        out_ref[...] = acc[:poses]


def partial_scores(totals, table, listing, volume, weights, y, square, step, noise, poses, block):
    planes, tiles, _, classes, width = volume.shape
    particles = y.shape[2] // 2
    bank = weights.shape[0]
    grid_spec = pltpu.PrefetchScalarGridSpec(
        num_scalar_prefetch=3,
        grid=(tiles // block,),
        in_specs=[
            pl.BlockSpec((planes, block, 2, classes, width), lambda t, *_: (0, t, 0, 0, 0)),
            pl.BlockSpec(weights.shape, lambda t, *_: (0, 0, 0), pipeline_mode=pl.Buffered(1)),
            pl.BlockSpec((block, 2 * width, 2 * particles), lambda t, *_: (t, 0, 0)),
            pl.BlockSpec((block, width, 2 * particles), lambda t, *_: (t, 0, 0)),
            pl.BlockSpec((block, 2, NTRANS, width), lambda t, *_: (t, 0, 0, 0)),
            pl.BlockSpec((block, 1, width), lambda t, *_: (t, 0, 0)),
        ],
        out_specs=pl.BlockSpec((poses, classes, NTRANS * particles), lambda t, *_: (0, 0, 0)),
        scratch_shapes=[pltpu.VMEM((poses + 1, classes, NTRANS * particles), F32)],
    )

    def body(*refs):
        score_kernel(bits_of(bank), bits_of(planes), *refs)

    return pl.pallas_call(
        body,
        grid_spec=grid_spec,
        out_shape=jax.ShapeDtypeStruct((poses, classes, NTRANS * particles), F32),
        compiler_params=pltpu.CompilerParams(vmem_limit_bytes=56 << 20),
        name="score",
    )(totals, table, listing, volume, weights, y, square, step, noise)


def spread_kernel(weight_bits, plane_bits, together, place_ref, total_ref, table_ref, list_ref, term_ref, weight_ref, y_ref, square_ref, step_ref, *refs):
    *piece_refs, own_ref, other_ref, posterior_ref, evidence_ref, scores, share, acc, sems = refs
    block = pl.program_id(0)
    tiles = y_ref.shape[0]
    width = square_ref.shape[2]
    poses, classes = scores.shape[0], scores.shape[1]
    n = term_ref.shape[1]
    half = own_ref.shape[0]
    rows = 2 * CHUNK * classes
    most = tiles * poses // CHUNK
    total = total_ref[block]

    @pl.when(block == 0)
    def _():
        copies = []
        for i, piece in enumerate(piece_refs):
            copies.append(pltpu.make_async_copy(piece, scores.at[pl.ds(place_ref[i], piece.shape[0])], sems.at[i]))
        for copy in copies:
            copy.start()
        for copy in copies:
            copy.wait()
        term = term_ref[...]

        def largest(p, best):
            for j in range(NTRANS):
                best = jnp.maximum(best, scores[p, :, j * n : (j + 1) * n] + term)
            return best

        best = lax.fori_loop(0, poses, largest, jnp.full((classes, n), -jnp.inf, F32))
        peak = jnp.max(best, axis=0, keepdims=True)

        def mass(p, totals):
            values = [jnp.exp((scores[p, :, j * n : (j + 1) * n] + term) - peak) for j in range(NTRANS)]
            for j in range(NTRANS):
                scores[p, :, j * n : (j + 1) * n] = values[j]
            for value in values:
                totals = totals + value
            return totals

        class_mass = lax.fori_loop(0, poses, mass, jnp.zeros((classes, n), F32))
        mass_total = jnp.sum(class_mass, axis=0, keepdims=True)
        posterior_ref[...] = class_mass / mass_total
        evidence_ref[...] = peak + jnp.log(mass_total)
        factor = jnp.broadcast_to(poses / mass_total, (classes, n))

        def normal(p, carry):
            values = [scores[p, :, j * n : (j + 1) * n] * factor for j in range(NTRANS)]
            every = values[0]
            for value in values[1:]:
                every = every + value
            for j, value in enumerate(values + [every]):
                high = value.astype(BF16).astype(F32)
                share[p, :, j * n : (j + 1) * n] = jnp.concatenate([high, value - high], axis=0).astype(BF16)
            return carry

        lax.fori_loop(0, poses, normal, 0)

    def entry(g):
        code = table_ref[block * most + g]
        return code >> bits_of(tiles), code & ((1 << bits_of(tiles)) - 1)

    def pairs(r):
        return jnp.concatenate(
            [r[2 * s * classes : (2 * s + 1) * classes] + r[(2 * s + 1) * classes : (2 * s + 2) * classes] for s in range(CHUNK)], axis=0
        )

    def gather(g):
        start, tt = entry(g)
        pose = [list_ref[start + s] >> (weight_bits + plane_bits) for s in range(CHUNK)]
        real = imag = None
        for first in range(0, NTRANS, together):
            steps = range(first, first + together)
            left = jnp.concatenate([share[pose[s], :, j * n : (j + 1) * n] for j in steps for s in range(CHUNK)], axis=0)
            every = jnp.dot(jnp.concatenate([left, left], axis=1), y_ref[tt], preferred_element_type=F32)
            for j in steps:
                r = pairs(every[(j - first) * rows : (j - first + 1) * rows])
                cosine, sine = step_ref[tt, 0, j : j + 1, :], step_ref[tt, 1, j : j + 1, :]
                moved = (r[:, :width] * cosine + r[:, width:] * sine, r[:, width:] * cosine - r[:, :width] * sine)
                real, imag = moved if real is None else (real + moved[0], imag + moved[1])
        left = jnp.concatenate([share[pose[s], :, NTRANS * n :] for s in range(CHUNK)], axis=0)
        power = pairs(jnp.dot(jnp.concatenate([left, left], axis=1), square_ref[tt], preferred_element_type=F32))
        return real, imag, power

    def scatter(g, sums):
        start, tt = entry(g)
        results, plane = [], []
        for s in range(CHUNK):
            code = list_ref[start + s]
            chosen = code & ((1 << weight_bits) - 1)
            plane.append((code >> weight_bits) & ((1 << plane_bits) - 1))
            value = jnp.concatenate([part[s * classes : (s + 1) * classes] for part in sums], axis=0)
            high = value.astype(BF16).astype(F32)
            both = jnp.concatenate([high, value - high], axis=0).astype(BF16)
            results.append(halves_sum(jnp.dot(both, weight_ref[chosen], preferred_element_type=F32)))
        for s in range(CHUNK):
            acc[plane[s], tt] += results[s]

    def chunk(g, sums):
        following = gather(g)
        scatter(jnp.maximum(g - 1, 0), sums)
        return following

    acc[...] = jnp.zeros_like(acc)
    nothing = jnp.zeros((CHUNK * classes, width), F32)
    sums = lax.fori_loop(0, total, chunk, (nothing, nothing, nothing))
    scatter(jnp.maximum(total - 1, 0), sums)
    own_ref[...] = acc[:half].reshape(own_ref.shape)
    other_ref[...] = acc[half : 2 * half].reshape(own_ref.shape)


def spread(places, totals, table, listing, pieces, term, weights, y, square, step, planes, block):
    poses, classes = sum(piece.shape[0] for piece in pieces), pieces[0].shape[1]
    tiles, particles, width = square.shape[0], square.shape[1] // 2, square.shape[2]
    bank = weights.shape[0]
    half = planes // 2
    part = pl.BlockSpec((half, block, 3, classes, width), lambda t, *_: (0, t, 0, 0, 0))
    grid_spec = pltpu.PrefetchScalarGridSpec(
        num_scalar_prefetch=4,
        grid=(tiles // block,),
        in_specs=[
            pl.BlockSpec(term.shape, lambda t, *_: (0, 0)),
            pl.BlockSpec(weights.shape, lambda t, *_: (0, 0, 0), pipeline_mode=pl.Buffered(1)),
            pl.BlockSpec((block, 2 * particles, 2 * width), lambda t, *_: (t, 0, 0)),
            pl.BlockSpec((block, 2 * particles, width), lambda t, *_: (t, 0, 0)),
            pl.BlockSpec((block, 2, NTRANS, width), lambda t, *_: (t, 0, 0, 0)),
        ]
        + [pl.BlockSpec(memory_space=pl.ANY)] * len(pieces),
        out_specs=[part, part, pl.BlockSpec((classes, particles), lambda t, *_: (0, 0)), pl.BlockSpec((1, particles), lambda t, *_: (0, 0))],
        scratch_shapes=[
            pltpu.VMEM((poses, classes, NTRANS * particles), F32),
            pltpu.VMEM((poses, 2 * classes, (NTRANS + 1) * particles), BF16),
            pltpu.VMEM((planes + 1, block, 3 * classes, width), F32),
            pltpu.SemaphoreType.DMA((len(pieces),)),
        ],
    )

    def body(*refs):
        spread_kernel(bits_of(bank), bits_of(planes + 1), TOGETHER, *refs)

    shape = jax.ShapeDtypeStruct((half, tiles, 3, classes, width), F32)
    return pl.pallas_call(
        body,
        grid_spec=grid_spec,
        out_shape=[shape, shape, jax.ShapeDtypeStruct((classes, particles), F32), jax.ShapeDtypeStruct((1, particles), F32)],
        compiler_params=pltpu.CompilerParams(vmem_limit_bytes=58 << 20),
        name="spread",
    )(places, totals, table, listing, term, weights, y, square, step, *pieces)


def gather_all(x, names):
    size = math.prod(lax.axis_size(name) for name in names)
    return lax.all_to_all(jnp.broadcast_to(x[None], (size, *x.shape)), names, 0, 0, tiled=True)


def square_routes():
    return [(0, 1), (1, 0), (2, 3), (3, 2)], [(0, 2), (2, 0), (1, 3), (3, 1)]


def scatter_sum(x):
    slabs = lax.axis_size("vol")
    own = x.shape[0] // slabs
    if slabs != 4 or own % 2:
        x = x.reshape(slabs, own, *x.shape[1:])
        return jnp.sum(lax.all_to_all(x, "vol", 0, 0, tiled=True), axis=0)
    along_x, along_y = square_routes()
    slab = lax.axis_index("vol")
    at_x, at_y = slab % 2, slab // 2
    x = x.reshape(2, 2, 2, own // 2, *x.shape[1:])

    def pick(values, index, axis):
        return lax.dynamic_index_in_dim(values, index, axis, keepdims=False)

    one, two = x[:, :, 0], x[:, :, 1]
    one = pick(one, at_x, 1) + lax.ppermute(pick(one, 1 - at_x, 1), "vol", along_x)
    two = pick(two, at_y, 0) + lax.ppermute(pick(two, 1 - at_y, 0), "vol", along_y)
    one = pick(one, at_y, 0) + lax.ppermute(pick(one, 1 - at_y, 0), "vol", along_y)
    two = pick(two, at_x, 0) + lax.ppermute(pick(two, 1 - at_x, 0), "vol", along_x)
    return jnp.concatenate([one, two])


def exchange(x):
    slabs, orients = lax.axis_size("vol"), lax.axis_size("orient")
    own = x.shape[0]
    if slabs != 4 or own % 2:
        return [lax.all_gather(x, ("vol", "orient"), tiled=True)], jnp.zeros((1,), jnp.int32)
    along_x, along_y = square_routes()
    ring = [(i, (i + 1) % orients) for i in range(orients)]
    slab, orient = lax.axis_index("vol"), lax.axis_index("orient")
    pieces, places = [], []
    for hop in range(orients):
        origin = jnp.mod(orient - hop, orients)
        following = lax.ppermute(x, "orient", ring) if hop + 1 < orients else None
        from_x, from_y = lax.ppermute(x, "vol", along_x), lax.ppermute(x, "vol", along_y)
        corner = [lax.ppermute(from_x[: own // 2], "vol", along_y), lax.ppermute(from_y[own // 2 :], "vol", along_x)]
        pieces += [x, from_x, from_y, *corner]
        for source, shift in ((slab, 0), (slab ^ 1, 0), (slab ^ 2, 0), (slab ^ 3, 0), (slab ^ 3, own // 2)):
            places.append((source * orients + origin) * own + shift)
        x = following
    return pieces, jnp.stack(places).astype(jnp.int32)


def shards(volume, weight_bank, tile_slab, tile_plane, tile_weight, particles, ctf, noise_weight, offsets, earlier_class, pose_free_term):
    slabs, orients, parts = lax.axis_size("vol"), lax.axis_size("orient"), lax.axis_size("dp")
    slab, orient, part = lax.axis_index("vol"), lax.axis_index("orient"), lax.axis_index("dp")
    planes, tiles, _, classes, width = volume.shape
    bank = weight_bank.shape[0]
    local_poses = tile_plane.shape[0]
    group = slabs * local_poses
    block = divisor(tiles, 5)

    named = jnp.stack([tile_slab[:, :, 0], tile_plane, tile_weight])
    named = gather_all(named, ("vol", "orient"))

    prior, step = phase_tables(tiles, width)
    options = prior.shape[1] // 2
    pick = [(offsets[:, axis : axis + 1] + REACH == jnp.arange(options, dtype=jnp.int32)[None]).astype(F32) for axis in (0, 1)]
    x, c = particles.transpose(1, 2, 0, 3), ctf.transpose(1, 0, 2)
    turned_y, turned_square = prepare(x, c, pick[0], pick[1], prior, block, True)
    high, low = rounded(weight_bank)
    ahead = jnp.concatenate([high, low], axis=2)
    weight_bits = bits_of(bank)
    named = named.reshape(slabs, orients, 3, local_poses, tiles)
    own = lax.dynamic_index_in_dim(named, orient, axis=1, keepdims=False)
    own = own.transpose(1, 0, 2, 3).reshape(3, group, tiles)
    pose = jnp.arange(group, dtype=jnp.int32)[:, None]
    shift = weight_bits + bits_of(planes)
    code = (pose << shift) | (own[1] << weight_bits) | own[2]
    listing, counts = compact(own[0] == slab, code, group << shift)

    every = named.transpose(2, 0, 1, 3, 4).reshape(3, slabs * orients * local_poses, tiles)
    reach = planes // orients
    half = reach // parts
    pose = jnp.arange(every.shape[1], dtype=jnp.int32)[:, None]
    place = jnp.mod(every[1] - orient * reach - part * half, reach)
    shift = weight_bits + bits_of(reach + 1)
    code = (pose << shift) | (place << weight_bits) | every[2]
    mask = (every[0] == slab) & (every[1] // reach == orient)
    back_listing, back_counts = compact(mask, code, reach << weight_bits)

    table, totals = chunk_table(counts, group, block)
    back_table, back_totals = chunk_table(back_counts, every.shape[1], block)
    scores = partial_scores(totals, table, listing, volume, ahead, turned_y, turned_square, step, noise_weight[:, None, :], group, block)
    scores = scatter_sum(scores)
    pieces, places = exchange(scores)

    weight_bank, x, c, _ = lax.optimization_barrier((weight_bank, x, c, scores))
    y, square = prepare(x, c, pick[0], pick[1], prior, block, False)
    high, low = rounded(weight_bank.transpose(0, 2, 1))
    back = jnp.concatenate([high, low], axis=2)
    term = jnp.where(earlier_class[None, :] == jnp.arange(classes, dtype=jnp.int32)[:, None], PREVIOUS_REWARD, 0.0)
    term = term + pose_free_term[None, :]
    mine, other, posterior, evidence = spread(places, back_totals, back_table, back_listing, pieces, term, back, y, square, step, reach, block)
    numerator = mine + lax.ppermute(other, "dp", [(0, 1), (1, 0)])
    return numerator, posterior.T, evidence[0]


def solution(mesh):
    in_specs = (
        P("vol", None, None, None, None),
        P(),
        P(("vol", "orient"), None, None),
        P(("vol", "orient"), None),
        P(("vol", "orient"), None),
        P("dp", None, None, None),
        P("dp", None, None),
        P(),
        P("dp", None),
        P("dp"),
        P("dp"),
    )
    out_specs = (P(("vol", "orient", "dp"), None, None, None, None), P("dp", None), P("dp"))
    return jax.shard_map(shards, mesh=mesh, in_specs=in_specs, out_specs=out_specs, check_vma=False)
```

```python
import math

import jax
import jax.numpy as jnp
import numpy as np
from jax import lax
from jax.experimental import pallas as pl
from jax.experimental.pallas import tpu as pltpu
from jax.sharding import PartitionSpec as P

SIDE = 128
NTRANS = 9
REACH = 3
PREVIOUS_REWARD = 1.5
CHUNK = 8
F32 = jnp.float32
BF16 = jnp.bfloat16


def phase_tables(tile_count, tile_width):
    pixel = np.arange(tile_count * tile_width).reshape(tile_count, tile_width)
    half_width = SIDE // 2 + 1
    freq_x = pixel % half_width
    row = pixel // half_width
    freq_y = np.where(row < SIDE // 2, row, row - SIDE)

    def pair(freq, steps):
        turns = np.mod(freq[:, None, :] * np.asarray(steps)[None, :, None], SIDE)
        angle = turns * (2.0 * math.pi / SIDE)
        return np.concatenate([np.cos(angle), np.sin(angle)], axis=2)

    steps = list(range(-REACH, REACH + 1)) + [0]
    prior = np.concatenate([pair(freq_x, steps), pair(freq_y, steps)], axis=1)
    j = np.arange(NTRANS)
    turns = np.mod(
        freq_x[:, None, :] * (j % 3 - 1)[None, :, None] + freq_y[:, None, :] * (j // 3 - 1)[None, :, None],
        SIDE,
    )
    angle = turns * (2.0 * math.pi / SIDE)
    step = np.stack([np.cos(angle), np.sin(angle)], axis=1)
    terms, rest = [], prior
    for _ in range(3):
        terms.append(rest.astype(np.float32).astype(BF16))
        rest = rest - terms[-1].astype(np.float64)
    x_part, y_part = slice(0, len(steps)), slice(len(steps), None)
    prior = np.concatenate([term[:, part] for part in (x_part, y_part) for term in terms], axis=1)
    return prior, step.astype(np.float32)


def divisor(count, most):
    return max(d for d in range(1, most + 1) if count % d == 0)


def split(x):
    high = x.astype(BF16)
    return high, (x - high.astype(F32)).astype(BF16)


def tree(join, values):
    while len(values) > 1:
        values = [join(*values[i : i + 2]) if i + 1 < len(values) else values[i] for i in range(0, len(values), 2)]
    return values[0]


def halves_sum(r):
    m, n = r.shape[0] // 2, r.shape[1] // 2
    return (r[:m, :n] + r[m:, :n]) + (r[:m, n:] + r[m:, n:])


def bits_of(count):
    return max(1, (count - 1).bit_length())


def compact(mask, code, spare):
    poses = mask.shape[0]
    order = jnp.arange(poses, dtype=jnp.int32)
    before = (order[:, None] > order[None, :]).astype(BF16)
    rank = jnp.dot(before, mask.astype(BF16), preferred_element_type=F32).astype(jnp.int32)
    rank = jnp.where(mask, rank, -1)
    hit = rank[None, :, :] == order[:, None, None]
    listing = jnp.sum(jnp.where(hit, (code - spare)[None], 0), axis=1) + spare
    return listing.T.reshape(-1), jnp.sum(mask.astype(jnp.int32), axis=0)


def chunk_table(counts, poses, block):
    chunks = ((counts + CHUNK - 1) // CHUNK).reshape(-1, block)
    place = jnp.arange(block, dtype=jnp.int32)
    end = jnp.sum(jnp.where(place[:, None] <= place[None, :], chunks[:, :, None], 0), axis=1)
    g = jnp.arange(block * poses // CHUNK, dtype=jnp.int32)[None, :, None]
    tile = jnp.minimum(jnp.sum((g >= end[:, None, :]).astype(jnp.int32), axis=2), block - 1)
    first = jnp.sum(jnp.where(place == tile[:, :, None], (end - chunks)[:, None, :], 0), axis=2)
    step = jnp.minimum(jnp.maximum(g[:, :, 0] - first, 0), poses // CHUNK - 1)
    start = (jnp.arange(chunks.shape[0], dtype=jnp.int32)[:, None] * block + tile) * poses + step * CHUNK
    return ((start << bits_of(block)) | tile).reshape(-1), end[:, -1]


def prepare_kernel(x_ref, ctf_ref, pick_x_ref, pick_y_ref, prior_ref, y_ref, square_ref, turned_y_ref, turned_square_ref):
    count = x_ref.shape[0]
    width = x_ref.shape[3]
    particles = x_ref.shape[2]
    options = pick_x_ref.shape[1]
    for tt in range(count):
        ex = jnp.dot(pick_x_ref[...], prior_ref[tt, :options], preferred_element_type=F32)
        ey = jnp.dot(pick_y_ref[...], prior_ref[tt, options:], preferred_element_type=F32)
        cx, sx, cy, sy = ex[:, :width], ex[:, width:], ey[:, :width], ey[:, width:]
        cosine = cx * cy - sx * sy
        sine = sx * cy + cx * sy
        ctf = ctf_ref[tt]
        real, imag = x_ref[tt, 0] * ctf, x_ref[tt, 1] * ctf
        moved = jnp.concatenate([real * cosine + imag * sine, imag * cosine - real * sine], axis=1)
        for source, plain, turned in ((moved, y_ref, turned_y_ref), (ctf * ctf, square_ref, turned_square_ref)):
            high, low = split(source)
            plain[tt, :particles, :] = high
            plain[tt, particles:, :] = low
            high, low = split(source.T)
            turned[tt, :, :particles] = high
            turned[tt, :, particles:] = low


def prepare(x, ctf, pick_x, pick_y, prior, block):
    tiles, _, particles, width = x.shape
    options = pick_x.shape[1]
    shapes = [(2 * particles, 2 * width), (2 * particles, width), (2 * width, 2 * particles), (width, 2 * particles)]
    return pl.pallas_call(
        prepare_kernel,
        grid=(tiles // block,),
        in_specs=[
            pl.BlockSpec((block, 2, particles, width), lambda t: (t, 0, 0, 0)),
            pl.BlockSpec((block, particles, width), lambda t: (t, 0, 0)),
            pl.BlockSpec((particles, options), lambda t: (0, 0)),
            pl.BlockSpec((particles, options), lambda t: (0, 0)),
            pl.BlockSpec((block, 2 * options, 2 * width), lambda t: (t, 0, 0)),
        ],
        out_specs=[pl.BlockSpec((block, *shape), lambda t: (t, 0, 0)) for shape in shapes],
        out_shape=[jax.ShapeDtypeStruct((tiles, *shape), BF16) for shape in shapes],
        compiler_params=pltpu.CompilerParams(vmem_limit_bytes=40 << 20),
        cost_estimate=pl.CostEstimate(flops=tiles * particles * width * 100, bytes_accessed=tiles * particles * width * 24, transcendentals=0),
        name="prepare",
    )(x, ctf, pick_x, pick_y, prior)


def score_kernel(weight_bits, plane_bits, total_ref, table_ref, list_ref, volume_ref, weight_ref, y_ref, square_ref, step_ref, noise_ref, out_ref, acc, bank):
    block = pl.program_id(0)
    tiles = y_ref.shape[0]
    width = square_ref.shape[1]
    n = square_ref.shape[2] // 2
    classes = volume_ref.shape[3]
    poses = out_ref.shape[0]
    rows = CHUNK * classes
    most = tiles * poses // CHUNK
    total = total_ref[block]

    @pl.when(block == 0)
    def _():
        acc[...] = jnp.zeros_like(acc)

        def halve(w, carry):
            bank[w] = jnp.concatenate(split(weight_ref[w]), axis=1)
            return carry

        lax.fori_loop(0, bank.shape[0], halve, 0, unroll=2)

    def entry(g):
        code = table_ref[block * most + g]
        return code >> bits_of(tiles), code & ((1 << bits_of(tiles)) - 1)

    def project(g):
        start, tt = entry(g)
        real, imag = [], []
        for s in range(CHUNK):
            code = list_ref[start + s]
            chosen = code & ((1 << weight_bits) - 1)
            plane = (code >> weight_bits) & ((1 << plane_bits) - 1)
            high, low = split(volume_ref[plane, tt].reshape(2 * classes, width))
            r = halves_sum(jnp.dot(jnp.concatenate([high, low], axis=0), bank[chosen], preferred_element_type=F32))
            real.append(r[:classes])
            imag.append(r[classes:])
        return jnp.concatenate(real, axis=0), jnp.concatenate(imag, axis=0)

    def chunk(g, slices):
        real, imag = slices
        following = project(jnp.minimum(g + 1, total - 1))
        start, tt = entry(g)
        pose = [list_ref[start + s] >> (weight_bits + plane_bits) for s in range(CHUNK)]
        noise = noise_ref[tt]
        high, low = split((real * real + imag * imag) * noise)
        norm = halves_sum(jnp.dot(jnp.concatenate([high, low], axis=0), square_ref[tt], preferred_element_type=F32))
        real, imag = real * (2.0 * noise), imag * (2.0 * noise)
        turned = []
        for j in range(NTRANS):
            cosine, sine = step_ref[tt, 0, j : j + 1, :], step_ref[tt, 1, j : j + 1, :]
            turned += split(jnp.concatenate([real * cosine - imag * sine, real * sine + imag * cosine], axis=1))
        r = jnp.dot(jnp.concatenate(turned, axis=0), y_ref[tt], preferred_element_type=F32)
        before = [acc[pose[s]] for s in range(CHUNK)]
        part = jnp.concatenate([halves_sum(r[2 * j * rows : 2 * (j + 1) * rows]) - norm for j in range(NTRANS)], axis=1)
        for s in range(CHUNK):
            acc[pose[s]] = before[s] + part[s * classes : (s + 1) * classes]
        return following

    lax.fori_loop(0, total, chunk, project(0))

    @pl.when(block == pl.num_programs(0) - 1)
    def _():
        out_ref[...] = acc[:poses]


def partial_scores(totals, table, listing, volume, weights, y, square, step, noise, poses, block):
    planes, tiles, _, classes, width = volume.shape
    particles = y.shape[2] // 2
    bank = weights.shape[0]
    grid_spec = pltpu.PrefetchScalarGridSpec(
        num_scalar_prefetch=3,
        grid=(tiles // block,),
        in_specs=[
            pl.BlockSpec((planes, block, 2, classes, width), lambda t, *_: (0, t, 0, 0, 0)),
            pl.BlockSpec(weights.shape, lambda t, *_: (0, 0, 0), pipeline_mode=pl.Buffered(1)),
            pl.BlockSpec((block, 2 * width, 2 * particles), lambda t, *_: (t, 0, 0)),
            pl.BlockSpec((block, width, 2 * particles), lambda t, *_: (t, 0, 0)),
            pl.BlockSpec((block, 2, NTRANS, width), lambda t, *_: (t, 0, 0, 0)),
            pl.BlockSpec((block, 1, width), lambda t, *_: (t, 0, 0)),
        ],
        out_specs=pl.BlockSpec((poses, classes, NTRANS * particles), lambda t, *_: (0, 0, 0)),
        scratch_shapes=[
            pltpu.VMEM((poses + 1, classes, NTRANS * particles), F32),
            pltpu.VMEM((weights.shape[0], weights.shape[1], 2 * weights.shape[2]), BF16),
        ],
    )

    def body(*refs):
        score_kernel(bits_of(bank), bits_of(planes), *refs)

    return pl.pallas_call(
        body,
        grid_spec=grid_spec,
        out_shape=jax.ShapeDtypeStruct((poses, classes, NTRANS * particles), F32),
        compiler_params=pltpu.CompilerParams(vmem_limit_bytes=56 << 20),
        name="score",
    )(totals, table, listing, volume, weights, y, square, step, noise)


def spread_kernel(weight_bits, plane_bits, together, place_ref, total_ref, table_ref, list_ref, term_ref, weight_ref, y_ref, square_ref, step_ref, *refs):
    *piece_refs, acc, posterior_ref, evidence_ref, scores, share, bank, sems = refs
    block = pl.program_id(0)
    tiles = y_ref.shape[0]
    width = square_ref.shape[2]
    poses, classes = scores.shape[0], scores.shape[1]
    n = term_ref.shape[1]
    rows = 2 * CHUNK * classes
    most = tiles * poses // CHUNK
    total = total_ref[block]

    @pl.when(block == 0)
    def _():
        copies = []
        for i, piece in enumerate(piece_refs):
            copies.append(pltpu.make_async_copy(piece, scores.at[pl.ds(place_ref[i], piece.shape[0])], sems.at[i]))
        for copy in copies:
            copy.start()

        def halve(w, carry):
            bank[w] = jnp.concatenate(split(weight_ref[w].T), axis=1)
            return carry

        lax.fori_loop(0, bank.shape[0], halve, 0, unroll=2)
        for copy in copies:
            copy.wait()
        term = term_ref[...]

        def largest(p, best):
            return jnp.maximum(best, tree(jnp.maximum, [scores[p, :, j * n : (j + 1) * n] + term for j in range(NTRANS)]))

        best = lax.fori_loop(0, poses, largest, jnp.full((classes, n), -jnp.inf, F32), unroll=4)
        peak = jnp.max(best, axis=0, keepdims=True)

        def mass(p, totals):
            values = [jnp.exp((scores[p, :, j * n : (j + 1) * n] + term) - peak) for j in range(NTRANS)]
            for j in range(NTRANS):
                scores[p, :, j * n : (j + 1) * n] = values[j]
            return totals + tree(jnp.add, values)

        class_mass = lax.fori_loop(0, poses, mass, jnp.zeros((classes, n), F32), unroll=2)
        mass_total = jnp.sum(class_mass, axis=0, keepdims=True)
        posterior_ref[...] = class_mass / mass_total
        evidence_ref[...] = peak + jnp.log(mass_total)
        factor = jnp.broadcast_to(poses / mass_total, (classes, n))

        def normal(p, carry):
            values = [scores[p, :, j * n : (j + 1) * n] * factor for j in range(NTRANS)]
            for j, value in enumerate(values + [tree(jnp.add, values)]):
                high = value.astype(BF16).astype(F32)
                share[p, :, j * n : (j + 1) * n] = jnp.concatenate([high, value - high], axis=0).astype(BF16)
            return carry

        lax.fori_loop(0, poses, normal, 0, unroll=2)

    def entry(g):
        code = table_ref[block * most + g]
        return code >> bits_of(tiles), code & ((1 << bits_of(tiles)) - 1)

    def pairs(r):
        return jnp.concatenate(
            [r[2 * s * classes : (2 * s + 1) * classes] + r[(2 * s + 1) * classes : (2 * s + 2) * classes] for s in range(CHUNK)], axis=0
        )

    def gather(g):
        start, tt = entry(g)
        pose = [list_ref[start + s] >> (weight_bits + plane_bits) for s in range(CHUNK)]
        real = imag = None
        for first in range(0, NTRANS, together):
            steps = range(first, first + together)
            left = jnp.concatenate([share[pose[s], :, j * n : (j + 1) * n] for j in steps for s in range(CHUNK)], axis=0)
            every = jnp.dot(jnp.concatenate([left, left], axis=1), y_ref[tt], preferred_element_type=F32)
            for j in steps:
                r = pairs(every[(j - first) * rows : (j - first + 1) * rows])
                cosine, sine = step_ref[tt, 0, j : j + 1, :], step_ref[tt, 1, j : j + 1, :]
                moved = (r[:, :width] * cosine + r[:, width:] * sine, r[:, width:] * cosine - r[:, :width] * sine)
                real, imag = moved if real is None else (real + moved[0], imag + moved[1])
        left = jnp.concatenate([share[pose[s], :, NTRANS * n :] for s in range(CHUNK)], axis=0)
        power = pairs(jnp.dot(jnp.concatenate([left, left], axis=1), square_ref[tt], preferred_element_type=F32))
        return real, imag, power

    def scatter(g, sums):
        start, tt = entry(g)
        results, plane = [], []
        for s in range(CHUNK):
            code = list_ref[start + s]
            chosen = code & ((1 << weight_bits) - 1)
            plane.append((code >> weight_bits) & ((1 << plane_bits) - 1))
            value = jnp.concatenate([part[s * classes : (s + 1) * classes] for part in sums], axis=0)
            high = value.astype(BF16).astype(F32)
            both = jnp.concatenate([high, value - high], axis=0).astype(BF16)
            results.append(halves_sum(jnp.dot(both, bank[chosen], preferred_element_type=F32)).reshape(3, classes, width))
        for s in range(CHUNK):
            acc[plane[s], tt] += results[s]

    def chunk(g, sums):
        following = gather(g)
        scatter(jnp.maximum(g - 1, 0), sums)
        return following

    acc[...] = jnp.zeros_like(acc)
    nothing = jnp.zeros((CHUNK * classes, width), F32)
    sums = lax.fori_loop(0, total, chunk, (nothing, nothing, nothing))
    scatter(jnp.maximum(total - 1, 0), sums)


def spread(places, totals, table, listing, pieces, term, weights, y, square, step, planes, block):
    poses, classes = sum(piece.shape[0] for piece in pieces), pieces[0].shape[1]
    tiles, particles, width = square.shape[0], square.shape[1] // 2, square.shape[2]
    bank = weights.shape[0]
    part = pl.BlockSpec((planes + 1, block, 3, classes, width), lambda t, *_: (0, t, 0, 0, 0))
    grid_spec = pltpu.PrefetchScalarGridSpec(
        num_scalar_prefetch=4,
        grid=(tiles // block,),
        in_specs=[
            pl.BlockSpec(term.shape, lambda t, *_: (0, 0)),
            pl.BlockSpec(weights.shape, lambda t, *_: (0, 0, 0), pipeline_mode=pl.Buffered(1)),
            pl.BlockSpec((block, 2 * particles, 2 * width), lambda t, *_: (t, 0, 0)),
            pl.BlockSpec((block, 2 * particles, width), lambda t, *_: (t, 0, 0)),
            pl.BlockSpec((block, 2, NTRANS, width), lambda t, *_: (t, 0, 0, 0)),
        ]
        + [pl.BlockSpec(memory_space=pl.ANY)] * len(pieces),
        out_specs=[part, pl.BlockSpec((classes, particles), lambda t, *_: (0, 0)), pl.BlockSpec((1, particles), lambda t, *_: (0, 0))],
        scratch_shapes=[
            pltpu.VMEM((poses, classes, NTRANS * particles), F32),
            pltpu.VMEM((poses, 2 * classes, (NTRANS + 1) * particles), BF16),
            pltpu.VMEM((bank, width, 2 * weights.shape[1]), BF16),
            pltpu.SemaphoreType.DMA((len(pieces),)),
        ],
    )

    def body(*refs):
        spread_kernel(bits_of(bank), bits_of(planes + 1), NTRANS, *refs)

    shape = jax.ShapeDtypeStruct((planes + 1, tiles, 3, classes, width), F32)
    return pl.pallas_call(
        body,
        grid_spec=grid_spec,
        out_shape=[shape, jax.ShapeDtypeStruct((classes, particles), F32), jax.ShapeDtypeStruct((1, particles), F32)],
        compiler_params=pltpu.CompilerParams(vmem_limit_bytes=58 << 20),
        name="spread",
    )(places, totals, table, listing, term, weights, y, square, step, *pieces)


def gather_all(x, names):
    size = math.prod(lax.axis_size(name) for name in names)
    return lax.all_to_all(jnp.broadcast_to(x[None], (size, *x.shape)), names, 0, 0, tiled=True)


def square_routes():
    return [(0, 1), (1, 0), (2, 3), (3, 2)], [(0, 2), (2, 0), (1, 3), (3, 1)]


def scatter_sum(x):
    slabs = lax.axis_size("vol")
    own = x.shape[0] // slabs
    if slabs != 4 or own % 2:
        x = x.reshape(slabs, own, *x.shape[1:])
        return jnp.sum(lax.all_to_all(x, "vol", 0, 0, tiled=True), axis=0)
    along_x, along_y = square_routes()
    slab = lax.axis_index("vol")
    at_x, at_y = slab % 2, slab // 2
    x = x.reshape(2, 2, 2, own // 2, *x.shape[1:])

    def pick(values, index, axis):
        return lax.dynamic_index_in_dim(values, index, axis, keepdims=False)

    one, two = x[:, :, 0], x[:, :, 1]
    one = pick(one, at_x, 1) + lax.ppermute(pick(one, 1 - at_x, 1), "vol", along_x)
    two = pick(two, at_y, 0) + lax.ppermute(pick(two, 1 - at_y, 0), "vol", along_y)
    one = pick(one, at_y, 0) + lax.ppermute(pick(one, 1 - at_y, 0), "vol", along_y)
    two = pick(two, at_x, 0) + lax.ppermute(pick(two, 1 - at_x, 0), "vol", along_x)
    return jnp.concatenate([one, two])


def exchange(x):
    slabs, orients = lax.axis_size("vol"), lax.axis_size("orient")
    own = x.shape[0]
    if slabs != 4:
        return [lax.all_gather(x, ("vol", "orient"), tiled=True)], jnp.zeros((1,), jnp.int32)
    along_x, along_y = square_routes()
    ring = [(i, (i + 1) % orients) for i in range(orients)]
    slab, orient = lax.axis_index("vol"), lax.axis_index("orient")
    pieces, places = [], []
    for hop in range(orients):
        origin = jnp.mod(orient - hop, orients)
        following = lax.ppermute(x, "orient", ring) if hop + 1 < orients else None
        from_x, from_y = lax.ppermute(x, "vol", along_x), lax.ppermute(x, "vol", along_y)
        corner = lax.ppermute(from_y, "vol", along_x) if hop % 2 else lax.ppermute(from_x, "vol", along_y)
        pieces += [x, from_x, from_y, corner]
        places += [((slab ^ side) * orients + origin) * own for side in range(4)]
        x = following
    return pieces, jnp.stack(places).astype(jnp.int32)


def shards(volume, weight_bank, tile_slab, tile_plane, tile_weight, particles, ctf, noise_weight, offsets, earlier_class, pose_free_term):
    slabs, orients, parts = lax.axis_size("vol"), lax.axis_size("orient"), lax.axis_size("dp")
    slab, orient, part = lax.axis_index("vol"), lax.axis_index("orient"), lax.axis_index("dp")
    planes, tiles, _, classes, width = volume.shape
    bank = weight_bank.shape[0]
    local_poses = tile_plane.shape[0]
    group = slabs * local_poses
    block = divisor(tiles, 13)

    named = jnp.stack([tile_slab[:, :, 0], tile_plane, tile_weight])
    named = gather_all(named, ("vol", "orient"))

    prior, step = phase_tables(tiles, width)
    options = prior.shape[1] // 2
    pick = [(offsets[:, axis : axis + 1] + REACH == jnp.arange(options, dtype=jnp.int32)[None] % (2 * REACH + 2)).astype(BF16) for axis in (0, 1)]
    x, c = particles.transpose(1, 2, 0, 3), ctf.transpose(1, 0, 2)
    y, square, turned_y, turned_square = prepare(x, c, pick[0], pick[1], prior, divisor(tiles, 5))
    weight_bits = bits_of(bank)
    named = named.reshape(slabs, orients, 3, local_poses, tiles)
    own = lax.dynamic_index_in_dim(named, orient, axis=1, keepdims=False)
    own = own.transpose(1, 0, 2, 3).reshape(3, group, tiles)
    pose = jnp.arange(group, dtype=jnp.int32)[:, None]
    shift = weight_bits + bits_of(planes)
    code = (pose << shift) | (own[1] << weight_bits) | own[2]
    listing, counts = compact(own[0] == slab, code, group << shift)

    every = named.transpose(2, 0, 1, 3, 4).reshape(3, slabs * orients * local_poses, tiles)
    reach = planes // orients
    half = reach // parts
    pose = jnp.arange(every.shape[1], dtype=jnp.int32)[:, None]
    place = jnp.mod(every[1] - orient * reach - part * half, reach)
    shift = weight_bits + bits_of(reach + 1)
    code = (pose << shift) | (place << weight_bits) | every[2]
    mask = (every[0] == slab) & (every[1] // reach == orient)
    back_listing, back_counts = compact(mask, code, reach << weight_bits)

    table, totals = chunk_table(counts, group, block)
    back_table, back_totals = chunk_table(back_counts, every.shape[1], block)
    scores = partial_scores(totals, table, listing, volume, weight_bank, turned_y, turned_square, step, noise_weight[:, None, :], group, block)
    scores = scatter_sum(scores)
    pieces, places = exchange(scores)

    term = jnp.where(earlier_class[None, :] == jnp.arange(classes, dtype=jnp.int32)[:, None], PREVIOUS_REWARD, 0.0)
    term = term + pose_free_term[None, :]
    sums, posterior, evidence = spread(places, back_totals, back_table, back_listing, pieces, term, weight_bank, y, square, step, reach, block)
    numerator = sums[:half] + lax.ppermute(sums[half : 2 * half], "dp", [(0, 1), (1, 0)])
    return numerator, posterior.T, evidence[0]


def solution(mesh):
    in_specs = (
        P("vol", None, None, None, None),
        P(),
        P(("vol", "orient"), None, None),
        P(("vol", "orient"), None),
        P(("vol", "orient"), None),
        P("dp", None, None, None),
        P("dp", None, None),
        P(),
        P("dp", None),
        P("dp"),
        P("dp"),
    )
    out_specs = (P(("vol", "orient", "dp"), None, None, None, None), P("dp", None), P("dp"))
    return jax.shard_map(shards, mesh=mesh, in_specs=in_specs, out_specs=out_specs, check_vma=False)
```

```python
import math

import jax
import jax.numpy as jnp
import numpy as np
from jax import lax
from jax.experimental import pallas as pl
from jax.experimental.pallas import tpu as pltpu
from jax.sharding import PartitionSpec as P

SIDE = 128
NTRANS = 9
REACH = 3
PREVIOUS_REWARD = 1.5
CHUNK = 8
F32 = jnp.float32
BF16 = jnp.bfloat16


def phase_tables(tile_count, tile_width):
    pixel = np.arange(tile_count * tile_width).reshape(tile_count, tile_width)
    half_width = SIDE // 2 + 1
    freq_x = pixel % half_width
    row = pixel // half_width
    freq_y = np.where(row < SIDE // 2, row, row - SIDE)

    def pair(freq, steps):
        turns = np.mod(freq[:, None, :] * np.asarray(steps)[None, :, None], SIDE)
        angle = turns * (2.0 * math.pi / SIDE)
        return np.concatenate([np.cos(angle), np.sin(angle)], axis=2)

    steps = list(range(-REACH, REACH + 1)) + [0]
    prior = np.concatenate([pair(freq_x, steps), pair(freq_y, steps)], axis=1)
    j = np.arange(NTRANS)
    turns = np.mod(
        freq_x[:, None, :] * (j % 3 - 1)[None, :, None] + freq_y[:, None, :] * (j // 3 - 1)[None, :, None],
        SIDE,
    )
    angle = turns * (2.0 * math.pi / SIDE)
    step = np.stack([np.cos(angle), np.sin(angle)], axis=1)
    terms, rest = [], prior
    for _ in range(3):
        terms.append(rest.astype(np.float32).astype(BF16))
        rest = rest - terms[-1].astype(np.float64)
    x_part, y_part = slice(0, len(steps)), slice(len(steps), None)
    prior = np.concatenate([term[:, part] for part in (x_part, y_part) for term in terms], axis=1)
    return prior, step.astype(np.float32)


def divisor(count, most):
    return max(d for d in range(1, most + 1) if count % d == 0)


def split(x):
    high = x.astype(BF16)
    return high, (x - high.astype(F32)).astype(BF16)


def tree(join, values):
    while len(values) > 1:
        values = [join(*values[i : i + 2]) if i + 1 < len(values) else values[i] for i in range(0, len(values), 2)]
    return values[0]


def halves_sum(r):
    m, n = r.shape[0] // 2, r.shape[1] // 2
    return (r[:m, :n] + r[m:, :n]) + (r[:m, n:] + r[m:, n:])


def bits_of(count):
    return max(1, (count - 1).bit_length())


def compact(mask, code, spare):
    poses = mask.shape[0]
    order = jnp.arange(poses, dtype=jnp.int32)
    before = (order[:, None] > order[None, :]).astype(BF16)
    rank = jnp.dot(before, mask.astype(BF16), preferred_element_type=F32).astype(jnp.int32)
    rank = jnp.where(mask, rank, -1)
    hit = rank[None, :, :] == order[:, None, None]
    listing = jnp.sum(jnp.where(hit, (code - spare)[None], 0), axis=1) + spare
    return listing.T.reshape(-1), jnp.sum(mask.astype(jnp.int32), axis=0)


def chunk_table(counts, poses, block):
    chunks = ((counts + CHUNK - 1) // CHUNK).reshape(-1, block)
    place = jnp.arange(block, dtype=jnp.int32)
    end = jnp.sum(jnp.where(place[:, None] <= place[None, :], chunks[:, :, None], 0), axis=1)
    g = jnp.arange(block * poses // CHUNK, dtype=jnp.int32)[None, :, None]
    tile = jnp.minimum(jnp.sum((g >= end[:, None, :]).astype(jnp.int32), axis=2), block - 1)
    first = jnp.sum(jnp.where(place == tile[:, :, None], (end - chunks)[:, None, :], 0), axis=2)
    step = jnp.minimum(jnp.maximum(g[:, :, 0] - first, 0), poses // CHUNK - 1)
    start = (jnp.arange(chunks.shape[0], dtype=jnp.int32)[:, None] * block + tile) * poses + step * CHUNK
    return ((start << bits_of(block)) | tile).reshape(-1), end[:, -1]


def prepare_kernel(x_ref, ctf_ref, pick_x_ref, pick_y_ref, prior_ref, y_ref, square_ref, turned_y_ref, turned_square_ref):
    particles, count, _, width = x_ref.shape
    options = pick_x_ref.shape[1]
    for tt in range(count):
        ex = jnp.dot(pick_x_ref[...], prior_ref[tt, :options], preferred_element_type=F32)
        ey = jnp.dot(pick_y_ref[...], prior_ref[tt, options:], preferred_element_type=F32)
        cx, sx, cy, sy = ex[:, :width], ex[:, width:], ey[:, :width], ey[:, width:]
        cosine = cx * cy - sx * sy
        sine = sx * cy + cx * sy
        ctf = ctf_ref[tt]
        real, imag = x_ref[:, tt, 0, :] * ctf, x_ref[:, tt, 1, :] * ctf
        moved = jnp.concatenate([real * cosine + imag * sine, imag * cosine - real * sine], axis=1)
        for source, plain, turned in ((moved, y_ref, turned_y_ref), (ctf * ctf, square_ref, turned_square_ref)):
            high, low = split(source)
            plain[tt, :particles, :] = high
            plain[tt, particles:, :] = low
            high, low = split(source.T)
            turned[tt, :, :particles] = high
            turned[tt, :, particles:] = low


def prepare(x, ctf, pick_x, pick_y, prior, block):
    particles, tiles, _, width = x.shape
    options = pick_x.shape[1]
    shapes = [(2 * particles, 2 * width), (2 * particles, width), (2 * width, 2 * particles), (width, 2 * particles)]
    return pl.pallas_call(
        prepare_kernel,
        grid=(tiles // block,),
        in_specs=[
            pl.BlockSpec((particles, block, 2, width), lambda t: (0, t, 0, 0)),
            pl.BlockSpec((block, particles, width), lambda t: (t, 0, 0)),
            pl.BlockSpec((particles, options), lambda t: (0, 0)),
            pl.BlockSpec((particles, options), lambda t: (0, 0)),
            pl.BlockSpec((block, 2 * options, 2 * width), lambda t: (t, 0, 0)),
        ],
        out_specs=[pl.BlockSpec((block, *shape), lambda t: (t, 0, 0)) for shape in shapes],
        out_shape=[jax.ShapeDtypeStruct((tiles, *shape), BF16) for shape in shapes],
        compiler_params=pltpu.CompilerParams(vmem_limit_bytes=60 << 20),
        cost_estimate=pl.CostEstimate(flops=tiles * particles * width * 100, bytes_accessed=tiles * particles * width * 24, transcendentals=0),
        name="prepare",
    )(x, ctf, pick_x, pick_y, prior)


def score_kernel(weight_bits, plane_bits, total_ref, table_ref, list_ref, volume_ref, weight_ref, y_ref, square_ref, step_ref, noise_ref, out_ref, acc, bank):
    block = pl.program_id(0)
    tiles = y_ref.shape[0]
    width = square_ref.shape[1]
    n = square_ref.shape[2] // 2
    classes = volume_ref.shape[3]
    poses = out_ref.shape[0]
    rows = CHUNK * classes
    most = tiles * poses // CHUNK
    total = total_ref[block]

    @pl.when(block == 0)
    def _():
        acc[...] = jnp.zeros_like(acc)

        def halve(w, carry):
            bank[w] = jnp.concatenate(split(weight_ref[w]), axis=1)
            return carry

        lax.fori_loop(0, bank.shape[0], halve, 0, unroll=2)

    def entry(g):
        code = table_ref[block * most + g]
        return code >> bits_of(tiles), code & ((1 << bits_of(tiles)) - 1)

    def project(g):
        start, tt = entry(g)
        real, imag = [], []
        for s in range(CHUNK):
            code = list_ref[start + s]
            chosen = code & ((1 << weight_bits) - 1)
            plane = (code >> weight_bits) & ((1 << plane_bits) - 1)
            high, low = split(volume_ref[plane, tt].reshape(2 * classes, width))
            r = halves_sum(jnp.dot(jnp.concatenate([high, low], axis=0), bank[chosen], preferred_element_type=F32))
            real.append(r[:classes])
            imag.append(r[classes:])
        return jnp.concatenate(real, axis=0), jnp.concatenate(imag, axis=0)

    def chunk(g, slices):
        real, imag = slices
        following = project(jnp.minimum(g + 1, total - 1))
        start, tt = entry(g)
        pose = [list_ref[start + s] >> (weight_bits + plane_bits) for s in range(CHUNK)]
        noise = noise_ref[tt]
        high, low = split((real * real + imag * imag) * noise)
        norm = halves_sum(jnp.dot(jnp.concatenate([high, low], axis=0), square_ref[tt], preferred_element_type=F32))
        real, imag = real * (2.0 * noise), imag * (2.0 * noise)
        parts = []
        for first in range(0, NTRANS, 3):
            turned = []
            for j in range(first, first + 3):
                cosine, sine = step_ref[tt, 0, j : j + 1, :], step_ref[tt, 1, j : j + 1, :]
                turned += split(jnp.concatenate([real * cosine - imag * sine, real * sine + imag * cosine], axis=1))
            r = jnp.dot(jnp.concatenate(turned, axis=0), y_ref[tt], preferred_element_type=F32)
            parts += [halves_sum(r[2 * j * rows : 2 * (j + 1) * rows]) - norm for j in range(3)]
        before = [acc[pose[s]] for s in range(CHUNK)]
        part = jnp.concatenate(parts, axis=1)
        for s in range(CHUNK):
            acc[pose[s]] = before[s] + part[s * classes : (s + 1) * classes]
        return following

    lax.fori_loop(0, total, chunk, project(0))

    @pl.when(block == pl.num_programs(0) - 1)
    def _():
        out_ref[...] = acc[:poses]


def partial_scores(totals, table, listing, volume, weights, y, square, step, noise, poses, block):
    planes, tiles, _, classes, width = volume.shape
    particles = y.shape[2] // 2
    bank = weights.shape[0]
    grid_spec = pltpu.PrefetchScalarGridSpec(
        num_scalar_prefetch=3,
        grid=(tiles // block,),
        in_specs=[
            pl.BlockSpec((planes, block, 2, classes, width), lambda t, *_: (0, t, 0, 0, 0)),
            pl.BlockSpec(weights.shape, lambda t, *_: (0, 0, 0), pipeline_mode=pl.Buffered(1)),
            pl.BlockSpec((block, 2 * width, 2 * particles), lambda t, *_: (t, 0, 0)),
            pl.BlockSpec((block, width, 2 * particles), lambda t, *_: (t, 0, 0)),
            pl.BlockSpec((block, 2, NTRANS, width), lambda t, *_: (t, 0, 0, 0)),
            pl.BlockSpec((block, 1, width), lambda t, *_: (t, 0, 0)),
        ],
        out_specs=pl.BlockSpec((poses, classes, NTRANS * particles), lambda t, *_: (0, 0, 0)),
        scratch_shapes=[
            pltpu.VMEM((poses + 1, classes, NTRANS * particles), F32),
            pltpu.VMEM((weights.shape[0], weights.shape[1], 2 * weights.shape[2]), BF16),
        ],
    )

    def body(*refs):
        score_kernel(bits_of(bank), bits_of(planes), *refs)

    return pl.pallas_call(
        body,
        grid_spec=grid_spec,
        out_shape=jax.ShapeDtypeStruct((poses, classes, NTRANS * particles), F32),
        compiler_params=pltpu.CompilerParams(vmem_limit_bytes=56 << 20),
        name="score",
    )(totals, table, listing, volume, weights, y, square, step, noise)


def spread_kernel(weight_bits, plane_bits, together, place_ref, total_ref, table_ref, list_ref, term_ref, weight_ref, y_ref, square_ref, step_ref, *refs):
    *piece_refs, acc, posterior_ref, evidence_ref, scores, share, bank, sems = refs
    block = pl.program_id(0)
    tiles = y_ref.shape[0]
    width = square_ref.shape[2]
    poses, classes = scores.shape[0], scores.shape[1]
    n = term_ref.shape[1]
    rows = 2 * CHUNK * classes
    most = tiles * poses // CHUNK
    total = total_ref[block]

    @pl.when(block == 0)
    def _():
        copies = []
        for i, piece in enumerate(piece_refs):
            copies.append(pltpu.make_async_copy(piece, scores.at[pl.ds(place_ref[i], piece.shape[0])], sems.at[i]))
        for copy in copies:
            copy.start()

        def halve(w, carry):
            bank[w] = jnp.concatenate(split(weight_ref[w].T), axis=1)
            return carry

        lax.fori_loop(0, bank.shape[0], halve, 0, unroll=2)
        for copy in copies:
            copy.wait()
        term = term_ref[...]

        def largest(p, best):
            return jnp.maximum(best, tree(jnp.maximum, [scores[p, :, j * n : (j + 1) * n] + term for j in range(NTRANS)]))

        best = lax.fori_loop(0, poses, largest, jnp.full((classes, n), -jnp.inf, F32), unroll=4)
        peak = jnp.max(best, axis=0, keepdims=True)

        def mass(p, totals):
            values = [jnp.exp((scores[p, :, j * n : (j + 1) * n] + term) - peak) for j in range(NTRANS)]
            for j in range(NTRANS):
                scores[p, :, j * n : (j + 1) * n] = values[j]
            return totals + tree(jnp.add, values)

        class_mass = lax.fori_loop(0, poses, mass, jnp.zeros((classes, n), F32), unroll=2)
        mass_total = jnp.sum(class_mass, axis=0, keepdims=True)
        posterior_ref[...] = class_mass / mass_total
        evidence_ref[...] = peak + jnp.log(mass_total)
        factor = jnp.broadcast_to(poses / mass_total, (classes, n))

        def normal(p, carry):
            values = [scores[p, :, j * n : (j + 1) * n] * factor for j in range(NTRANS)]
            for j, value in enumerate(values + [tree(jnp.add, values)]):
                high = value.astype(BF16).astype(F32)
                share[p, :, j * n : (j + 1) * n] = jnp.concatenate([high, value - high], axis=0).astype(BF16)
            return carry

        lax.fori_loop(0, poses, normal, 0, unroll=2)

    def entry(g):
        code = table_ref[block * most + g]
        return code >> bits_of(tiles), code & ((1 << bits_of(tiles)) - 1)

    def pairs(r):
        return jnp.concatenate(
            [r[2 * s * classes : (2 * s + 1) * classes] + r[(2 * s + 1) * classes : (2 * s + 2) * classes] for s in range(CHUNK)], axis=0
        )

    def gather(g):
        start, tt = entry(g)
        pose = [list_ref[start + s] >> (weight_bits + plane_bits) for s in range(CHUNK)]
        real = imag = None
        for first in range(0, NTRANS, together):
            steps = range(first, first + together)
            left = jnp.concatenate([share[pose[s], :, j * n : (j + 1) * n] for j in steps for s in range(CHUNK)], axis=0)
            every = jnp.dot(jnp.concatenate([left, left], axis=1), y_ref[tt], preferred_element_type=F32)
            for j in steps:
                r = pairs(every[(j - first) * rows : (j - first + 1) * rows])
                cosine, sine = step_ref[tt, 0, j : j + 1, :], step_ref[tt, 1, j : j + 1, :]
                moved = (r[:, :width] * cosine + r[:, width:] * sine, r[:, width:] * cosine - r[:, :width] * sine)
                real, imag = moved if real is None else (real + moved[0], imag + moved[1])
        left = jnp.concatenate([share[pose[s], :, NTRANS * n :] for s in range(CHUNK)], axis=0)
        power = pairs(jnp.dot(jnp.concatenate([left, left], axis=1), square_ref[tt], preferred_element_type=F32))
        return real, imag, power

    def scatter(g, sums):
        start, tt = entry(g)
        results, plane = [], []
        for s in range(CHUNK):
            code = list_ref[start + s]
            chosen = code & ((1 << weight_bits) - 1)
            plane.append((code >> weight_bits) & ((1 << plane_bits) - 1))
            value = jnp.concatenate([part[s * classes : (s + 1) * classes] for part in sums], axis=0)
            high = value.astype(BF16).astype(F32)
            both = jnp.concatenate([high, value - high], axis=0).astype(BF16)
            results.append(halves_sum(jnp.dot(both, bank[chosen], preferred_element_type=F32)).reshape(3, classes, width))
        for s in range(CHUNK):
            acc[plane[s], tt] += results[s]

    def chunk(g, sums):
        following = gather(g)
        scatter(jnp.maximum(g - 1, 0), sums)
        return following

    acc[...] = jnp.zeros_like(acc)
    nothing = jnp.zeros((CHUNK * classes, width), F32)
    sums = lax.fori_loop(0, total, chunk, (nothing, nothing, nothing))
    scatter(jnp.maximum(total - 1, 0), sums)


def spread(places, totals, table, listing, pieces, term, weights, y, square, step, planes, block):
    poses, classes = sum(piece.shape[0] for piece in pieces), pieces[0].shape[1]
    tiles, particles, width = square.shape[0], square.shape[1] // 2, square.shape[2]
    bank = weights.shape[0]
    part = pl.BlockSpec((planes + 1, block, 3, classes, width), lambda t, *_: (0, t, 0, 0, 0))
    grid_spec = pltpu.PrefetchScalarGridSpec(
        num_scalar_prefetch=4,
        grid=(tiles // block,),
        in_specs=[
            pl.BlockSpec(term.shape, lambda t, *_: (0, 0)),
            pl.BlockSpec(weights.shape, lambda t, *_: (0, 0, 0), pipeline_mode=pl.Buffered(1)),
            pl.BlockSpec((block, 2 * particles, 2 * width), lambda t, *_: (t, 0, 0)),
            pl.BlockSpec((block, 2 * particles, width), lambda t, *_: (t, 0, 0)),
            pl.BlockSpec((block, 2, NTRANS, width), lambda t, *_: (t, 0, 0, 0)),
        ]
        + [pl.BlockSpec(memory_space=pl.ANY)] * len(pieces),
        out_specs=[part, pl.BlockSpec((classes, particles), lambda t, *_: (0, 0)), pl.BlockSpec((1, particles), lambda t, *_: (0, 0))],
        scratch_shapes=[
            pltpu.VMEM((poses, classes, NTRANS * particles), F32),
            pltpu.VMEM((poses, 2 * classes, (NTRANS + 1) * particles), BF16),
            pltpu.VMEM((bank, width, 2 * weights.shape[1]), BF16),
            pltpu.SemaphoreType.DMA((len(pieces),)),
        ],
    )

    def body(*refs):
        spread_kernel(bits_of(bank), bits_of(planes + 1), NTRANS, *refs)

    shape = jax.ShapeDtypeStruct((planes + 1, tiles, 3, classes, width), F32)
    return pl.pallas_call(
        body,
        grid_spec=grid_spec,
        out_shape=[shape, jax.ShapeDtypeStruct((classes, particles), F32), jax.ShapeDtypeStruct((1, particles), F32)],
        compiler_params=pltpu.CompilerParams(vmem_limit_bytes=58 << 20),
        name="spread",
    )(places, totals, table, listing, term, weights, y, square, step, *pieces)


def gather_all(x, names):
    size = math.prod(lax.axis_size(name) for name in names)
    return lax.all_to_all(jnp.broadcast_to(x[None], (size, *x.shape)), names, 0, 0, tiled=True)


def square_routes():
    return [(0, 1), (1, 0), (2, 3), (3, 2)], [(0, 2), (2, 0), (1, 3), (3, 1)]


def scatter_sum(x):
    slabs = lax.axis_size("vol")
    own = x.shape[0] // slabs
    if slabs != 4 or own % 2:
        x = x.reshape(slabs, own, *x.shape[1:])
        return jnp.sum(lax.all_to_all(x, "vol", 0, 0, tiled=True), axis=0)
    along_x, along_y = square_routes()
    slab = lax.axis_index("vol")
    at_x, at_y = slab % 2, slab // 2
    x = x.reshape(2, 2, 2, own // 2, *x.shape[1:])

    def pick(values, index, axis):
        return lax.dynamic_index_in_dim(values, index, axis, keepdims=False)

    one, two = x[:, :, 0], x[:, :, 1]
    one = pick(one, at_x, 1) + lax.ppermute(pick(one, 1 - at_x, 1), "vol", along_x)
    two = pick(two, at_y, 0) + lax.ppermute(pick(two, 1 - at_y, 0), "vol", along_y)
    one = pick(one, at_y, 0) + lax.ppermute(pick(one, 1 - at_y, 0), "vol", along_y)
    two = pick(two, at_x, 0) + lax.ppermute(pick(two, 1 - at_x, 0), "vol", along_x)
    return jnp.concatenate([one, two])


def exchange(x):
    slabs, orients = lax.axis_size("vol"), lax.axis_size("orient")
    own = x.shape[0]
    if slabs != 4:
        return [lax.all_gather(x, ("vol", "orient"), tiled=True)], jnp.zeros((1,), jnp.int32)
    along_x, along_y = square_routes()
    ring = [(i, (i + 1) % orients) for i in range(orients)]
    slab, orient = lax.axis_index("vol"), lax.axis_index("orient")
    pieces, places = [], []
    for hop in range(orients):
        origin = jnp.mod(orient - hop, orients)
        following = lax.ppermute(x, "orient", ring) if hop + 1 < orients else None
        from_x, from_y = lax.ppermute(x, "vol", along_x), lax.ppermute(x, "vol", along_y)
        corner = lax.ppermute(from_y, "vol", along_x) if hop % 2 else lax.ppermute(from_x, "vol", along_y)
        pieces += [x, from_x, from_y, corner]
        places += [((slab ^ side) * orients + origin) * own for side in range(4)]
        x = following
    return pieces, jnp.stack(places).astype(jnp.int32)


def shards(volume, weight_bank, tile_slab, tile_plane, tile_weight, particles, ctf, noise_weight, offsets, earlier_class, pose_free_term):
    slabs, orients, parts = lax.axis_size("vol"), lax.axis_size("orient"), lax.axis_size("dp")
    slab, orient, part = lax.axis_index("vol"), lax.axis_index("orient"), lax.axis_index("dp")
    planes, tiles, _, classes, width = volume.shape
    bank = weight_bank.shape[0]
    local_poses = tile_plane.shape[0]
    group = slabs * local_poses
    block = divisor(tiles, 13)

    named = jnp.stack([tile_slab[:, :, 0], tile_plane, tile_weight])
    named = gather_all(named, ("vol", "orient"))

    prior, step = phase_tables(tiles, width)
    options = prior.shape[1] // 2
    pick = [(offsets[:, axis : axis + 1] + REACH == jnp.arange(options, dtype=jnp.int32)[None] % (2 * REACH + 2)).astype(BF16) for axis in (0, 1)]
    y, square, turned_y, turned_square = prepare(particles, ctf.transpose(1, 0, 2), pick[0], pick[1], prior, block)
    weight_bits = bits_of(bank)
    named = named.reshape(slabs, orients, 3, local_poses, tiles)
    own = lax.dynamic_index_in_dim(named, orient, axis=1, keepdims=False)
    own = own.transpose(1, 0, 2, 3).reshape(3, group, tiles)
    pose = jnp.arange(group, dtype=jnp.int32)[:, None]
    shift = weight_bits + bits_of(planes)
    code = (pose << shift) | (own[1] << weight_bits) | own[2]
    listing, counts = compact(own[0] == slab, code, group << shift)

    every = named.transpose(2, 0, 1, 3, 4).reshape(3, slabs * orients * local_poses, tiles)
    reach = planes // orients
    half = reach // parts
    pose = jnp.arange(every.shape[1], dtype=jnp.int32)[:, None]
    place = jnp.mod(every[1] - orient * reach - part * half, reach)
    shift = weight_bits + bits_of(reach + 1)
    code = (pose << shift) | (place << weight_bits) | every[2]
    mask = (every[0] == slab) & (every[1] // reach == orient)
    back_listing, back_counts = compact(mask, code, reach << weight_bits)

    table, totals = chunk_table(counts, group, block)
    back_table, back_totals = chunk_table(back_counts, every.shape[1], block)
    scores = partial_scores(totals, table, listing, volume, weight_bank, turned_y, turned_square, step, noise_weight[:, None, :], group, block)
    scores = scatter_sum(scores)
    pieces, places = exchange(scores)

    term = jnp.where(earlier_class[None, :] == jnp.arange(classes, dtype=jnp.int32)[:, None], PREVIOUS_REWARD, 0.0)
    term = term + pose_free_term[None, :]
    sums, posterior, evidence = spread(places, back_totals, back_table, back_listing, pieces, term, weight_bank, y, square, step, reach, block)
    numerator = sums[:half] + lax.ppermute(sums[half : 2 * half], "dp", [(0, 1), (1, 0)])
    return numerator, posterior.T, evidence[0]


def solution(mesh):
    in_specs = (
        P("vol", None, None, None, None),
        P(),
        P(("vol", "orient"), None, None),
        P(("vol", "orient"), None),
        P(("vol", "orient"), None),
        P("dp", None, None, None),
        P("dp", None, None),
        P(),
        P("dp", None),
        P("dp"),
        P("dp"),
    )
    out_specs = (P(("vol", "orient", "dp"), None, None, None, None), P("dp", None), P("dp"))
    return jax.shard_map(shards, mesh=mesh, in_specs=in_specs, out_specs=out_specs, check_vma=False)
```

```python
import math

import jax
import jax.numpy as jnp
import numpy as np
from jax import lax
from jax.experimental import pallas as pl
from jax.experimental.pallas import tpu as pltpu
from jax.sharding import PartitionSpec as P

SIDE = 128
NTRANS = 9
REACH = 3
PREVIOUS_REWARD = 1.5
CHUNK = 8
F32 = jnp.float32
BF16 = jnp.bfloat16


def phase_tables(tile_count, tile_width):
    pixel = np.arange(tile_count * tile_width).reshape(tile_count, tile_width)
    half_width = SIDE // 2 + 1
    freq_x = pixel % half_width
    row = pixel // half_width
    freq_y = np.where(row < SIDE // 2, row, row - SIDE)

    def pair(freq, steps):
        turns = np.mod(freq[:, None, :] * np.asarray(steps)[None, :, None], SIDE)
        angle = turns * (2.0 * math.pi / SIDE)
        return np.concatenate([np.cos(angle), np.sin(angle)], axis=2)

    steps = list(range(-REACH, REACH + 1)) + [0]
    prior = np.concatenate([pair(freq_x, steps), pair(freq_y, steps)], axis=1)
    j = np.arange(NTRANS)
    turns = np.mod(
        freq_x[:, None, :] * (j % 3 - 1)[None, :, None] + freq_y[:, None, :] * (j // 3 - 1)[None, :, None],
        SIDE,
    )
    angle = turns * (2.0 * math.pi / SIDE)
    step = np.stack([np.cos(angle), np.sin(angle)], axis=1)
    terms, rest = [], prior
    for _ in range(3):
        terms.append(rest.astype(np.float32).astype(BF16))
        rest = rest - terms[-1].astype(np.float64)
    x_part, y_part = slice(0, len(steps)), slice(len(steps), None)
    prior = np.concatenate([term[:, part] for part in (x_part, y_part) for term in terms], axis=1)
    return prior, step.astype(np.float32)


def divisor(count, most):
    return max(d for d in range(1, most + 1) if count % d == 0)


def split(x):
    high = x.astype(BF16)
    return high, (x - high.astype(F32)).astype(BF16)


def tree(join, values):
    while len(values) > 1:
        values = [join(*values[i : i + 2]) if i + 1 < len(values) else values[i] for i in range(0, len(values), 2)]
    return values[0]


def halves_sum(r):
    m, n = r.shape[0] // 2, r.shape[1] // 2
    return (r[:m, :n] + r[m:, :n]) + (r[:m, n:] + r[m:, n:])


def bits_of(count):
    return max(1, (count - 1).bit_length())


def compact(mask, code, spare):
    poses = mask.shape[0]
    order = jnp.arange(poses, dtype=jnp.int32)
    before = (order[:, None] > order[None, :]).astype(BF16)
    rank = jnp.dot(before, mask.astype(BF16), preferred_element_type=F32).astype(jnp.int32)
    rank = jnp.where(mask, rank, -1)
    hit = rank[None, :, :] == order[:, None, None]
    listing = jnp.sum(jnp.where(hit, (code - spare)[None], 0), axis=1) + spare
    return listing.T.reshape(-1), jnp.sum(mask.astype(jnp.int32), axis=0)


def chunk_table(counts, poses, block):
    chunks = ((counts + CHUNK - 1) // CHUNK).reshape(-1, block)
    place = jnp.arange(block, dtype=jnp.int32)
    end = jnp.sum(jnp.where(place[:, None] <= place[None, :], chunks[:, :, None], 0), axis=1)
    g = jnp.arange(block * poses // CHUNK, dtype=jnp.int32)[None, :, None]
    tile = jnp.minimum(jnp.sum((g >= end[:, None, :]).astype(jnp.int32), axis=2), block - 1)
    first = jnp.sum(jnp.where(place == tile[:, :, None], (end - chunks)[:, None, :], 0), axis=2)
    step = jnp.minimum(jnp.maximum(g[:, :, 0] - first, 0), poses // CHUNK - 1)
    start = (jnp.arange(chunks.shape[0], dtype=jnp.int32)[:, None] * block + tile) * poses + step * CHUNK
    return ((start << bits_of(block)) | tile).reshape(-1), end[:, -1]


def prepare_kernel(x_ref, ctf_ref, pick_x_ref, pick_y_ref, prior_ref, y_ref, square_ref, turned_y_ref, turned_square_ref):
    particles, count, _, width = x_ref.shape
    options = pick_x_ref.shape[1]
    for tt in range(count):
        ex = jnp.dot(pick_x_ref[...], prior_ref[tt, :options], preferred_element_type=F32)
        ey = jnp.dot(pick_y_ref[...], prior_ref[tt, options:], preferred_element_type=F32)
        cx, sx, cy, sy = ex[:, :width], ex[:, width:], ey[:, :width], ey[:, width:]
        cosine = cx * cy - sx * sy
        sine = sx * cy + cx * sy
        ctf = ctf_ref[tt]
        real, imag = x_ref[:, tt, 0, :] * ctf, x_ref[:, tt, 1, :] * ctf
        moved = jnp.concatenate([real * cosine + imag * sine, imag * cosine - real * sine], axis=1)
        for source, plain, turned in ((moved, y_ref, turned_y_ref), (ctf * ctf, square_ref, turned_square_ref)):
            high, low = split(source)
            plain[tt, :particles, :] = high
            plain[tt, particles:, :] = low
            high, low = split(source.T)
            turned[tt, :, :particles] = high
            turned[tt, :, particles:] = low


def prepare(x, ctf, pick_x, pick_y, prior, block):
    particles, tiles, _, width = x.shape
    options = pick_x.shape[1]
    shapes = [(2 * particles, 2 * width), (2 * particles, width), (2 * width, 2 * particles), (width, 2 * particles)]
    return pl.pallas_call(
        prepare_kernel,
        grid=(tiles // block,),
        in_specs=[
            pl.BlockSpec((particles, block, 2, width), lambda t: (0, t, 0, 0)),
            pl.BlockSpec((block, particles, width), lambda t: (t, 0, 0)),
            pl.BlockSpec((particles, options), lambda t: (0, 0)),
            pl.BlockSpec((particles, options), lambda t: (0, 0)),
            pl.BlockSpec((block, 2 * options, 2 * width), lambda t: (t, 0, 0)),
        ],
        out_specs=[pl.BlockSpec((block, *shape), lambda t: (t, 0, 0)) for shape in shapes],
        out_shape=[jax.ShapeDtypeStruct((tiles, *shape), BF16) for shape in shapes],
        compiler_params=pltpu.CompilerParams(vmem_limit_bytes=60 << 20),
        cost_estimate=pl.CostEstimate(flops=tiles * particles * width * 100, bytes_accessed=tiles * particles * width * 24, transcendentals=0),
        name="prepare",
    )(x, ctf, pick_x, pick_y, prior)


def score_kernel(weight_bits, plane_bits, total_ref, table_ref, list_ref, volume_ref, weight_ref, y_ref, square_ref, step_ref, noise_ref, out_ref, acc, bank):
    block = pl.program_id(0)
    tiles = y_ref.shape[0]
    width = square_ref.shape[1]
    n = square_ref.shape[2] // 2
    classes = volume_ref.shape[3]
    poses = out_ref.shape[0]
    rows = CHUNK * classes
    most = tiles * poses // CHUNK
    total = total_ref[block]

    @pl.when(block == 0)
    def _():
        acc[...] = jnp.zeros_like(acc)

        def halve(w, carry):
            bank[w] = jnp.concatenate(split(weight_ref[w]), axis=1)
            return carry

        lax.fori_loop(0, bank.shape[0], halve, 0, unroll=8)

    def entry(g):
        code = table_ref[block * most + g]
        return code >> bits_of(tiles), code & ((1 << bits_of(tiles)) - 1)

    def project(g):
        start, tt = entry(g)
        real, imag = [], []
        for s in range(CHUNK):
            code = list_ref[start + s]
            chosen = code & ((1 << weight_bits) - 1)
            plane = (code >> weight_bits) & ((1 << plane_bits) - 1)
            high, low = split(volume_ref[plane, tt].reshape(2 * classes, width))
            r = halves_sum(jnp.dot(jnp.concatenate([high, low], axis=0), bank[chosen], preferred_element_type=F32))
            real.append(r[:classes])
            imag.append(r[classes:])
        return jnp.concatenate(real, axis=0), jnp.concatenate(imag, axis=0)

    def chunk(g, slices):
        real, imag = slices
        following = project(jnp.minimum(g + 1, total - 1))
        start, tt = entry(g)
        pose = [list_ref[start + s] >> (weight_bits + plane_bits) for s in range(CHUNK)]
        noise = noise_ref[tt]
        high, low = split((real * real + imag * imag) * noise)
        norm = halves_sum(jnp.dot(jnp.concatenate([high, low], axis=0), square_ref[tt], preferred_element_type=F32))
        real, imag = real * (2.0 * noise), imag * (2.0 * noise)
        parts = []
        for first in range(0, NTRANS, 3):
            turned = []
            for j in range(first, first + 3):
                cosine, sine = step_ref[tt, 0, j : j + 1, :], step_ref[tt, 1, j : j + 1, :]
                turned += split(jnp.concatenate([real * cosine - imag * sine, real * sine + imag * cosine], axis=1))
            r = jnp.dot(jnp.concatenate(turned, axis=0), y_ref[tt], preferred_element_type=F32)
            parts += [halves_sum(r[2 * j * rows : 2 * (j + 1) * rows]) - norm for j in range(3)]
        before = [acc[pose[s]] for s in range(CHUNK)]
        part = jnp.concatenate(parts, axis=1)
        for s in range(CHUNK):
            acc[pose[s]] = before[s] + part[s * classes : (s + 1) * classes]
        return following

    lax.fori_loop(0, total, chunk, project(0))

    @pl.when(block == pl.num_programs(0) - 1)
    def _():
        out_ref[...] = acc[:poses]


def partial_scores(totals, table, listing, volume, weights, y, square, step, noise, poses, block):
    planes, tiles, _, classes, width = volume.shape
    particles = y.shape[2] // 2
    bank = weights.shape[0]
    grid_spec = pltpu.PrefetchScalarGridSpec(
        num_scalar_prefetch=3,
        grid=(tiles // block,),
        in_specs=[
            pl.BlockSpec((planes, block, 2, classes, width), lambda t, *_: (0, t, 0, 0, 0)),
            pl.BlockSpec(weights.shape, lambda t, *_: (0, 0, 0), pipeline_mode=pl.Buffered(1)),
            pl.BlockSpec((block, 2 * width, 2 * particles), lambda t, *_: (t, 0, 0)),
            pl.BlockSpec((block, width, 2 * particles), lambda t, *_: (t, 0, 0)),
            pl.BlockSpec((block, 2, NTRANS, width), lambda t, *_: (t, 0, 0, 0)),
            pl.BlockSpec((block, 1, width), lambda t, *_: (t, 0, 0)),
        ],
        out_specs=pl.BlockSpec((poses, classes, NTRANS * particles), lambda t, *_: (0, 0, 0)),
        scratch_shapes=[
            pltpu.VMEM((poses + 1, classes, NTRANS * particles), F32),
            pltpu.VMEM((weights.shape[0], weights.shape[1], 2 * weights.shape[2]), BF16),
        ],
    )

    def body(*refs):
        score_kernel(bits_of(bank), bits_of(planes), *refs)

    return pl.pallas_call(
        body,
        grid_spec=grid_spec,
        out_shape=jax.ShapeDtypeStruct((poses, classes, NTRANS * particles), F32),
        compiler_params=pltpu.CompilerParams(vmem_limit_bytes=56 << 20),
        name="score",
    )(totals, table, listing, volume, weights, y, square, step, noise)


def spread_kernel(weight_bits, plane_bits, together, place_ref, total_ref, table_ref, list_ref, term_ref, weight_ref, y_ref, square_ref, step_ref, *refs):
    *piece_refs, acc, posterior_ref, evidence_ref, scores, share, bank, sems = refs
    block = pl.program_id(0)
    tiles = y_ref.shape[0]
    width = square_ref.shape[2]
    poses, classes = scores.shape[0], scores.shape[1]
    n = term_ref.shape[1]
    rows = 2 * CHUNK * classes
    most = tiles * poses // CHUNK
    total = total_ref[block]

    @pl.when(block == 0)
    def _():
        copies = []
        for i, piece in enumerate(piece_refs):
            copies.append(pltpu.make_async_copy(piece, scores.at[pl.ds(place_ref[i], piece.shape[0])], sems.at[i]))
        for copy in copies:
            copy.start()

        def halve(w, carry):
            bank[w] = jnp.concatenate(split(weight_ref[w].T), axis=1)
            return carry

        lax.fori_loop(0, bank.shape[0], halve, 0, unroll=8)
        for copy in copies:
            copy.wait()
        term = term_ref[...]

        def largest(p, best):
            return jnp.maximum(best, tree(jnp.maximum, [scores[p, :, j * n : (j + 1) * n] + term for j in range(NTRANS)]))

        best = lax.fori_loop(0, poses, largest, jnp.full((classes, n), -jnp.inf, F32), unroll=8)
        peak = jnp.max(best, axis=0, keepdims=True)

        def mass(p, totals):
            values = [jnp.exp((scores[p, :, j * n : (j + 1) * n] + term) - peak) for j in range(NTRANS)]
            for j in range(NTRANS):
                scores[p, :, j * n : (j + 1) * n] = values[j]
            return totals + tree(jnp.add, values)

        class_mass = lax.fori_loop(0, poses, mass, jnp.zeros((classes, n), F32), unroll=4)
        mass_total = jnp.sum(class_mass, axis=0, keepdims=True)
        posterior_ref[...] = class_mass / mass_total
        evidence_ref[...] = peak + jnp.log(mass_total)
        factor = jnp.broadcast_to(poses / mass_total, (classes, n))

        def normal(p, carry):
            values = [scores[p, :, j * n : (j + 1) * n] * factor for j in range(NTRANS)]
            for j, value in enumerate(values + [tree(jnp.add, values)]):
                high = value.astype(BF16).astype(F32)
                share[p, :, j * n : (j + 1) * n] = jnp.concatenate([high, value - high], axis=0).astype(BF16)
            return carry

        lax.fori_loop(0, poses, normal, 0, unroll=4)

    def entry(g):
        code = table_ref[block * most + g]
        return code >> bits_of(tiles), code & ((1 << bits_of(tiles)) - 1)

    def pairs(r):
        return jnp.concatenate(
            [r[2 * s * classes : (2 * s + 1) * classes] + r[(2 * s + 1) * classes : (2 * s + 2) * classes] for s in range(CHUNK)], axis=0
        )

    def gather(g):
        start, tt = entry(g)
        pose = [list_ref[start + s] >> (weight_bits + plane_bits) for s in range(CHUNK)]
        real = imag = None
        for first in range(0, NTRANS, together):
            steps = range(first, first + together)
            left = jnp.concatenate([share[pose[s], :, j * n : (j + 1) * n] for j in steps for s in range(CHUNK)], axis=0)
            every = jnp.dot(jnp.concatenate([left, left], axis=1), y_ref[tt], preferred_element_type=F32)
            for j in steps:
                r = pairs(every[(j - first) * rows : (j - first + 1) * rows])
                cosine, sine = step_ref[tt, 0, j : j + 1, :], step_ref[tt, 1, j : j + 1, :]
                moved = (r[:, :width] * cosine + r[:, width:] * sine, r[:, width:] * cosine - r[:, :width] * sine)
                real, imag = moved if real is None else (real + moved[0], imag + moved[1])
        left = jnp.concatenate([share[pose[s], :, NTRANS * n :] for s in range(CHUNK)], axis=0)
        power = pairs(jnp.dot(jnp.concatenate([left, left], axis=1), square_ref[tt], preferred_element_type=F32))
        return real, imag, power

    def scatter(g, sums):
        start, tt = entry(g)
        results, plane = [], []
        for s in range(CHUNK):
            code = list_ref[start + s]
            chosen = code & ((1 << weight_bits) - 1)
            plane.append((code >> weight_bits) & ((1 << plane_bits) - 1))
            value = jnp.concatenate([part[s * classes : (s + 1) * classes] for part in sums], axis=0)
            high = value.astype(BF16).astype(F32)
            both = jnp.concatenate([high, value - high], axis=0).astype(BF16)
            results.append(halves_sum(jnp.dot(both, bank[chosen], preferred_element_type=F32)).reshape(3, classes, width))
        for s in range(CHUNK):
            acc[plane[s], tt] += results[s]

    def chunk(g, sums):
        following = gather(g)
        scatter(jnp.maximum(g - 1, 0), sums)
        return following

    acc[...] = jnp.zeros_like(acc)
    nothing = jnp.zeros((CHUNK * classes, width), F32)
    sums = lax.fori_loop(0, total, chunk, (nothing, nothing, nothing))
    scatter(jnp.maximum(total - 1, 0), sums)


def spread(places, totals, table, listing, pieces, term, weights, y, square, step, planes, block):
    poses, classes = sum(piece.shape[0] for piece in pieces), pieces[0].shape[1]
    tiles, particles, width = square.shape[0], square.shape[1] // 2, square.shape[2]
    bank = weights.shape[0]
    part = pl.BlockSpec((planes + 1, block, 3, classes, width), lambda t, *_: (0, t, 0, 0, 0))
    grid_spec = pltpu.PrefetchScalarGridSpec(
        num_scalar_prefetch=4,
        grid=(tiles // block,),
        in_specs=[
            pl.BlockSpec(term.shape, lambda t, *_: (0, 0)),
            pl.BlockSpec(weights.shape, lambda t, *_: (0, 0, 0), pipeline_mode=pl.Buffered(1)),
            pl.BlockSpec((block, 2 * particles, 2 * width), lambda t, *_: (t, 0, 0)),
            pl.BlockSpec((block, 2 * particles, width), lambda t, *_: (t, 0, 0)),
            pl.BlockSpec((block, 2, NTRANS, width), lambda t, *_: (t, 0, 0, 0)),
        ]
        + [pl.BlockSpec(memory_space=pl.ANY)] * len(pieces),
        out_specs=[part, pl.BlockSpec((classes, particles), lambda t, *_: (0, 0)), pl.BlockSpec((1, particles), lambda t, *_: (0, 0))],
        scratch_shapes=[
            pltpu.VMEM((poses, classes, NTRANS * particles), F32),
            pltpu.VMEM((poses, 2 * classes, (NTRANS + 1) * particles), BF16),
            pltpu.VMEM((bank, width, 2 * weights.shape[1]), BF16),
            pltpu.SemaphoreType.DMA((len(pieces),)),
        ],
    )

    def body(*refs):
        spread_kernel(bits_of(bank), bits_of(planes + 1), NTRANS, *refs)

    shape = jax.ShapeDtypeStruct((planes + 1, tiles, 3, classes, width), F32)
    return pl.pallas_call(
        body,
        grid_spec=grid_spec,
        out_shape=[shape, jax.ShapeDtypeStruct((classes, particles), F32), jax.ShapeDtypeStruct((1, particles), F32)],
        compiler_params=pltpu.CompilerParams(vmem_limit_bytes=58 << 20),
        name="spread",
    )(places, totals, table, listing, term, weights, y, square, step, *pieces)


def gather_all(x, names):
    size = math.prod(lax.axis_size(name) for name in names)
    return lax.all_to_all(jnp.broadcast_to(x[None], (size, *x.shape)), names, 0, 0, tiled=True)


def square_routes():
    return [(0, 1), (1, 0), (2, 3), (3, 2)], [(0, 2), (2, 0), (1, 3), (3, 1)]


def scatter_sum(x):
    slabs = lax.axis_size("vol")
    own = x.shape[0] // slabs
    if slabs != 4 or own % 2:
        x = x.reshape(slabs, own, *x.shape[1:])
        return jnp.sum(lax.all_to_all(x, "vol", 0, 0, tiled=True), axis=0)
    along_x, along_y = square_routes()
    slab = lax.axis_index("vol")
    at_x, at_y = slab % 2, slab // 2
    x = x.reshape(2, 2, 2, own // 2, *x.shape[1:])

    def pick(values, index, axis):
        return lax.dynamic_index_in_dim(values, index, axis, keepdims=False)

    one, two = x[:, :, 0], x[:, :, 1]
    one = pick(one, at_x, 1) + lax.ppermute(pick(one, 1 - at_x, 1), "vol", along_x)
    two = pick(two, at_y, 0) + lax.ppermute(pick(two, 1 - at_y, 0), "vol", along_y)
    one = pick(one, at_y, 0) + lax.ppermute(pick(one, 1 - at_y, 0), "vol", along_y)
    two = pick(two, at_x, 0) + lax.ppermute(pick(two, 1 - at_x, 0), "vol", along_x)
    return jnp.concatenate([one, two])


def exchange(x):
    slabs, orients = lax.axis_size("vol"), lax.axis_size("orient")
    own = x.shape[0]
    if slabs != 4:
        return [lax.all_gather(x, ("vol", "orient"), tiled=True)], jnp.zeros((1,), jnp.int32)
    along_x, along_y = square_routes()
    ring = [(i, (i + 1) % orients) for i in range(orients)]
    slab, orient = lax.axis_index("vol"), lax.axis_index("orient")
    pieces, places = [], []
    for hop in range(orients):
        origin = jnp.mod(orient - hop, orients)
        following = lax.ppermute(x, "orient", ring) if hop + 1 < orients else None
        from_x, from_y = lax.ppermute(x, "vol", along_x), lax.ppermute(x, "vol", along_y)
        corner = lax.ppermute(from_y, "vol", along_x) if hop % 2 else lax.ppermute(from_x, "vol", along_y)
        pieces += [x, from_x, from_y, corner]
        places += [((slab ^ side) * orients + origin) * own for side in range(4)]
        x = following
    return pieces, jnp.stack(places).astype(jnp.int32)


def shards(volume, weight_bank, tile_slab, tile_plane, tile_weight, particles, ctf, noise_weight, offsets, earlier_class, pose_free_term):
    slabs, orients, parts = lax.axis_size("vol"), lax.axis_size("orient"), lax.axis_size("dp")
    slab, orient, part = lax.axis_index("vol"), lax.axis_index("orient"), lax.axis_index("dp")
    planes, tiles, _, classes, width = volume.shape
    bank = weight_bank.shape[0]
    local_poses = tile_plane.shape[0]
    group = slabs * local_poses
    block = divisor(tiles, 13)

    named = jnp.stack([tile_slab[:, :, 0], tile_plane, tile_weight])
    named = gather_all(named, ("vol", "orient"))

    prior, step = phase_tables(tiles, width)
    options = prior.shape[1] // 2
    pick = [(offsets[:, axis : axis + 1] + REACH == jnp.arange(options, dtype=jnp.int32)[None] % (2 * REACH + 2)).astype(BF16) for axis in (0, 1)]
    y, square, turned_y, turned_square = prepare(particles, ctf.transpose(1, 0, 2), pick[0], pick[1], prior, block)
    weight_bits = bits_of(bank)
    named = named.reshape(slabs, orients, 3, local_poses, tiles)
    own = lax.dynamic_index_in_dim(named, orient, axis=1, keepdims=False)
    own = own.transpose(1, 0, 2, 3).reshape(3, group, tiles)
    pose = jnp.arange(group, dtype=jnp.int32)[:, None]
    shift = weight_bits + bits_of(planes)
    code = (pose << shift) | (own[1] << weight_bits) | own[2]
    listing, counts = compact(own[0] == slab, code, group << shift)

    every = named.transpose(2, 0, 1, 3, 4).reshape(3, slabs * orients * local_poses, tiles)
    reach = planes // orients
    half = reach // parts
    pose = jnp.arange(every.shape[1], dtype=jnp.int32)[:, None]
    place = jnp.mod(every[1] - orient * reach - part * half, reach)
    shift = weight_bits + bits_of(reach + 1)
    code = (pose << shift) | (place << weight_bits) | every[2]
    mask = (every[0] == slab) & (every[1] // reach == orient)
    back_listing, back_counts = compact(mask, code, reach << weight_bits)

    table, totals = chunk_table(counts, group, block)
    back_table, back_totals = chunk_table(back_counts, every.shape[1], block)
    scores = partial_scores(totals, table, listing, volume, weight_bank, turned_y, turned_square, step, noise_weight[:, None, :], group, block)
    scores = scatter_sum(scores)
    pieces, places = exchange(scores)

    term = jnp.where(earlier_class[None, :] == jnp.arange(classes, dtype=jnp.int32)[:, None], PREVIOUS_REWARD, 0.0)
    term = term + pose_free_term[None, :]
    sums, posterior, evidence = spread(places, back_totals, back_table, back_listing, pieces, term, weight_bank, y, square, step, reach, block)
    numerator = sums[:half] + lax.ppermute(sums[half : 2 * half], "dp", [(0, 1), (1, 0)])
    return numerator, posterior.T, evidence[0]


def solution(mesh):
    in_specs = (
        P("vol", None, None, None, None),
        P(),
        P(("vol", "orient"), None, None),
        P(("vol", "orient"), None),
        P(("vol", "orient"), None),
        P("dp", None, None, None),
        P("dp", None, None),
        P(),
        P("dp", None),
        P("dp"),
        P("dp"),
    )
    out_specs = (P(("vol", "orient", "dp"), None, None, None, None), P("dp", None), P("dp"))
    return jax.shard_map(shards, mesh=mesh, in_specs=in_specs, out_specs=out_specs, check_vma=False)
```
